32 devices in a mesh: dp: 8 (over y, x, core), fsdp: 4 (over z).
Axes of the slice: x: 2, y: 2, z: 4, core: 2. Of those that a mesh axis runs over, the one named last changes fastest.
Arguments:
- tokens: bfloat16 [8, 1024, 2048], P('dp', 'fsdp'), may hold values from -6 to 6
- segments: int32 [8, 1024], P('dp'), may hold values from 0 to 5, never falling along the last dimension, each value on 1 to 512 neighbouring positions
- out_grad: bfloat16 [8, 1024, 2048], P('dp', 'fsdp'), may hold values from -6 to 6
- owners: int32 [384], replicated, may hold values from 0 to 31, as said below
- blocks: float32 [384, 256, 512], P(('dp', 'fsdp')), may hold values from -2 to 2
- first_moment: float32 [384, 256, 512], P(('dp', 'fsdp')), may hold values from -6 to 6
- second_moment: float32 [384, 256, 512], P(('dp', 'fsdp')), may hold values from 0.25 to 4
- left_bases: float32 [384, 256, 256], P(('dp', 'fsdp')), may hold values from -0.375 to 0.375
- right_bases: float32 [384, 512, 512], P(('dp', 'fsdp')), may hold values from -0.25 to 0.25
- vectors: float32 [24576], P(('dp', 'fsdp')), may hold values from -0.5 to 1.25
- vector_first: float32 [24576], P(('dp', 'fsdp')), may hold values from -6 to 6
- vector_second: float32 [24576], P(('dp', 'fsdp')), may hold values from 0.25 to 4
Outputs:
- out_tokens: bfloat16 [8, 1024, 2048], P('dp', 'fsdp')
- input_grad: float32 [8, 1024, 2048], P('dp', 'fsdp')
- block_grads: float32 [384, 256, 512], P(('dp', 'fsdp'))
- vector_grads: float32 [24576], P(('dp', 'fsdp'))
- new_blocks: float32 [384, 256, 512], P(('dp', 'fsdp'))
- new_first: float32 [384, 256, 512], P(('dp', 'fsdp'))
- new_second: float32 [384, 256, 512], P(('dp', 'fsdp'))
- block_copies: bfloat16 [384, 256, 512], P(('dp', 'fsdp'))
- new_vectors: float32 [24576], P(('dp', 'fsdp'))
- new_vector_first: float32 [24576], P(('dp', 'fsdp'))
- new_vector_second: float32 [24576], P(('dp', 'fsdp'))
- vector_copies: bfloat16 [24576], P(('dp', 'fsdp'))
- grad_norm: float32 [], replicated
- clip_factors: float32 [16], replicated
The draws below stay inside these ranges and needn't reach their ends.
Inputs may be any that keep to these rules, and one draw needn't show every extreme that they name: `owners`: each device index of the joined axis dp+fsdp owns exactly 12 blocks. `segments`: within a sequence the ids never fall; each of the 6 documents has 1 to 512 tokens, one exactly 512.
All inputs are finite; a program needn't handle non-finite values.
Results may differ from the reference program's by a relative error of at most 0.012.
Values may be sent and summed in bfloat16 or wider, within the bound.
No kernel may reach another device: no remote copies, remote signals or barrier semaphores. Data moves between devices by JAX's collectives and lax.ppermute only.
A program may use at most 512 MiB of HBM per device.

```python
import math
import jax
import jax.numpy as jnp
import numpy as np
from jax import lax

D = 2048
HEADS = 16
DH = 128
FF = 8192
LEN = 1024
BR = 256
BC = 512
SEQS = 8
NBLK = 384
BPD = 12
VEC = 24576


def owner_table(key):
    shuffled = jax.random.permutation(jax.random.fold_in(key, 17), NBLK).astype(jnp.int32)
    positions = jnp.zeros((NBLK,), jnp.int32).at[shuffled].set(jnp.arange(NBLK, dtype=jnp.int32))
    return positions // BPD


def draw_owners(key, part):
    return owner_table(key)


def draw_blocks(key, part):
    owners = owner_table(key)
    block_ids = jnp.arange(NBLK, dtype=jnp.int32)
    earlier = (owners[None, :] == owners[:, None]) & (block_ids[None, :] < block_ids[:, None])
    slot_of_block = owners * BPD + jnp.sum(earlier.astype(jnp.int32), axis=1)
    block_at_slot = jnp.zeros((NBLK,), jnp.int32).at[slot_of_block].set(block_ids)
    qkv_end = D // BR * (3 * D // BC)
    out_end = qkv_end + D // BR * (D // BC)
    up_end = out_end + D // BR * (FF // BC)
    spread = jnp.where(block_at_slot < qkv_end, D ** (-0.5), jnp.where(block_at_slot < out_end, 4.0 * D ** (-0.5), jnp.where(block_at_slot < up_end, D ** (-0.5), FF ** (-0.5))))
    values = jax.random.truncated_normal(jax.random.fold_in(key, 29), -4.0, 4.0, (NBLK, BR, BC), jnp.float32)
    return values * spread[:, None, None].astype(jnp.float32)


def draw_vectors(key, part):
    positions = jnp.arange(VEC, dtype=jnp.int32)
    noise = jax.random.uniform(jax.random.fold_in(key, 31), (VEC,), jnp.float32, -1.0, 1.0)
    kind_of = positions % 8
    gains = (positions < 8 * D) & ((kind_of == 0) | (kind_of == 5))
    return jnp.where(gains, 1.0 + 0.25 * noise, 0.5 * noise)


def block_levels(own_key, dims, cuts, low, top_value):
    def one(dim, blocks):
        draws = jax.random.uniform(jax.random.fold_in(jax.random.fold_in(own_key, 6), dim), (blocks,), jnp.float32, low / len(cuts), top_value / len(cuts))
        return jnp.repeat(jnp.exp(draws), dims[dim] // blocks).reshape((-1,) + (1,) * (len(dims) - dim - 1))

    loudness = one(*cuts[0])
    for cut in cuts[1:]:
        loudness = loudness * one(*cut)
    return loudness


def length_profile(count, total, reach, skew):
    loads = [(1 << 20) // math.isqrt(grade ** skew) + 1 for grade in range(2, count + 1)]
    spare, counts = total - reach - (count - 1), [1] * (count - 1)
    while spare > 0:
        candidates = [i for i in range(count - 1) if counts[i] < reach]
        whole, left = sum([loads[i] for i in candidates]), spare
        for i in candidates:
            extra = min(reach - counts[i], max(1, left * loads[i] // whole), spare)
            counts[i] = counts[i] + extra
            spare = spare - extra
    return np.array([reach] + counts)


def ragged(key, amount, total, bound, slope):
    if amount == 2:
        one = jax.random.randint(key, (), max(1, total - bound), min(bound, total - 1) + 1)
        return jnp.stack([one, total - one])
    tallies = jnp.asarray(length_profile(amount, total, bound, slope), jnp.int32)
    twos = (amount - 1) // 2
    giver, sink = tallies[1:1 + 2 * twos:2], tallies[2:2 + 2 * twos:2]
    slack = jnp.minimum(giver - 1, bound - sink)
    shifted = jax.random.randint(jax.random.fold_in(key, 1), (twos,), 0, 1 << 20) % (slack + 1)
    tallies = tallies.at[1:1 + 2 * twos:2].set(giver - shifted).at[2:2 + 2 * twos:2].set(sink + shifted)
    return tallies[jax.random.permutation(jax.random.fold_in(key, 2), amount)]


def bell_draw(own_key, shape, scale, limit, split=(), kind=jnp.bfloat16):
    gain = block_levels(own_key, shape, split, -0.22, 0.18) if split else 1.0
    values = jax.random.normal(own_key, shape, jnp.float32) * scale * gain
    return jnp.minimum(jnp.maximum(values, -limit), limit).astype(kind)


def setup_inputs(seed: int = 0) -> dict:
    key_of = jax.random.split(jax.random.key(seed), 13)
    return {
        "tokens": bell_draw(key_of[0], (SEQS, LEN, D), 1.0, 6.0, ((0, 8), (1, 4))),
        "segments": jax.vmap(lambda own: jnp.searchsorted(jnp.cumsum(ragged(own, 6, LEN, LEN // 2, 1)), jnp.arange(LEN), side="right"))(jax.random.split(key_of[1], SEQS)).reshape((SEQS, LEN)).astype(jnp.int32),
        "out_grad": bell_draw(key_of[2], (SEQS, LEN, D), 1.0, 6.0, ((0, 8), (1, 4))),
        "owners": draw_owners(jax.random.fold_in(key_of[12], 71), 0),
        "blocks": draw_blocks(jax.random.fold_in(key_of[12], 71), 0),
        "first_moment": bell_draw(key_of[5], (NBLK, BR, BC), 1.0, 6.0, ((0, 32),), jnp.float32),
        "second_moment": jnp.clip(jnp.exp(math.log(4.0) - 2.7725887 * jax.random.uniform(key_of[6], (NBLK, BR, BC), jnp.float32) ** block_levels(key_of[6], (NBLK, BR, BC), ((0, 32),), -0.2, 0.2)), 0.25, 4.0),
        "left_bases": bell_draw(key_of[7], (NBLK, BR, BR), BR ** -0.5, 0.375, ((0, 32),), jnp.float32),
        "right_bases": bell_draw(key_of[8], (NBLK, BC, BC), BC ** -0.5, 0.25, ((0, 32),), jnp.float32),
        "vectors": draw_vectors(jax.random.fold_in(key_of[12], 71), 0),
        "vector_first": bell_draw(key_of[10], (VEC,), 1.0, 6.0, ((0, 32),), jnp.float32),
        "vector_second": jnp.clip(jnp.exp(math.log(4.0) - 2.7725887 * jax.random.uniform(key_of[11], (VEC,), jnp.float32) ** block_levels(key_of[11], (VEC,), ((0, 32),), -0.2, 0.2)), 0.25, 4.0),
    }


HIGH = lax.Precision.HIGHEST
NEG = -1e+30

@jax.custom_vjp
def low(v):
    return lax.optimization_barrier(v.astype(jnp.bfloat16)).astype(jnp.float32)

@jax.custom_vjp
def low_back(v):
    return v

def low_keep(v):
    return (low(v), None)

def low_pass(kept, grad):
    return (grad,)

def back_keep(v):
    return (v, None)

def back_low(kept, grad):
    return (low(grad),)
low.defvjp(low_keep, low_pass)
low_back.defvjp(back_keep, back_low)

def layer_norm(hidden, gain_vector, shift_vector):
    average = lax.optimization_barrier(jnp.mean(hidden, axis=-1, keepdims=True))
    centred = hidden - average
    variance = lax.optimization_barrier(jnp.mean(centred * centred, axis=-1, keepdims=True))
    return centred * lax.rsqrt(variance + 1e-05) * gain_vector + shift_vector

def to_matrix(block_list, rows_all, cols_all):
    shaped = block_list.reshape(rows_all // BR, cols_all // BC, BR, BC)
    return shaped.transpose(0, 2, 1, 3).reshape(rows_all, cols_all)

def from_matrix(matrix):
    rows_all, cols_all = matrix.shape
    shaped = matrix.reshape(rows_all // BR, BR, cols_all // BC, BC)
    return shaped.transpose(0, 2, 1, 3).reshape(-1, BR, BC)

def split_blocks(blocks_by_id):
    qkv_end = D // BR * (3 * D // BC)
    out_end = qkv_end + D // BR * (D // BC)
    up_end = out_end + D // BR * (FF // BC)
    return (to_matrix(blocks_by_id[:qkv_end], D, 3 * D), to_matrix(blocks_by_id[qkv_end:out_end], D, D), to_matrix(blocks_by_id[out_end:up_end], D, FF), to_matrix(blocks_by_id[up_end:], FF, D))

def split_vectors(vector_all):
    feature_major = vector_all[:8 * D].reshape(D, 8)
    pieces = [feature_major[:, index_one] for index_one in range(8)]
    return pieces + [vector_all[8 * D:]]

def slot_tables(owners, per_owner):
    total_blocks = owners.shape[0]
    block_ids = jnp.arange(total_blocks, dtype=jnp.int32)
    earlier = (owners[None, :] == owners[:, None]) & (block_ids[None, :] < block_ids[:, None])
    slot_of_block = owners * per_owner + lax.optimization_barrier(jnp.sum(earlier.astype(jnp.int32), axis=1))
    block_at_slot = jnp.zeros((total_blocks,), jnp.int32).at[slot_of_block].set(block_ids)
    return (slot_of_block, block_at_slot)

def column_scale(block_ids, root_factor):
    per_row = 3 * D // BC
    qkv_total = D // BR * per_row
    columns = (block_ids % per_row)[:, None] * BC + jnp.arange(BC, dtype=jnp.int32)[None, :]
    head_of = columns % D // DH
    picked = lax.optimization_barrier(jnp.sum(jnp.where(head_of[..., None] == jnp.arange(HEADS, dtype=jnp.int32), root_factor, 0.0), axis=-1))
    inside = (block_ids < qkv_total)[:, None] & (columns < 2 * D)
    return jnp.where(inside, picked, 1.0)

def vector_scale(positions, root_factor):
    inside = (positions < 8 * D) & (positions % 8 == 2)
    head_of = positions // 8 // DH
    picked = lax.optimization_barrier(jnp.sum(jnp.where(head_of[:, None] == jnp.arange(HEADS, dtype=jnp.int32), root_factor, 0.0), axis=-1))
    return jnp.where(inside, picked, 1.0)

def rotate_in(matrix, left_basis, right_basis):
    left_done = jnp.einsum('bij,bik->bjk', left_basis, matrix, precision=HIGH, preferred_element_type=jnp.float32)
    return jnp.einsum('bjk,bkl->bjl', left_done, right_basis, precision=HIGH, preferred_element_type=jnp.float32)

def rotate_out(matrix, left_basis, right_basis):
    left_done = jnp.einsum('bij,bjk->bik', left_basis, matrix, precision=HIGH, preferred_element_type=jnp.float32)
    return jnp.einsum('bik,blk->bil', left_done, right_basis, precision=HIGH, preferred_element_type=jnp.float32)

def attend(query, keys, values, seg_ids):
    query4 = query.reshape(LEN, HEADS, DH)
    keys4 = keys.reshape(LEN, HEADS, DH)
    values4 = values.reshape(LEN, HEADS, DH)
    scores = jnp.einsum('qhd,khd->hqk', query4, keys4, precision=HIGH, preferred_element_type=jnp.float32) * DH ** (-0.5)
    scores = low_back(scores)
    positions = jnp.arange(LEN, dtype=jnp.int32)
    allowed = (positions[None, :] <= positions[:, None]) & (seg_ids[None, :] == seg_ids[:, None])
    masked = jnp.where(allowed[None], scores, NEG)
    log_total = jax.nn.logsumexp(masked, axis=-1, keepdims=True)
    probs = low(jnp.exp(masked - log_total))
    mixed = jnp.einsum('hqk,khd->qhd', probs, values4, precision=HIGH, preferred_element_type=jnp.float32)
    return (mixed.reshape(LEN, D), lax.optimization_barrier(jnp.max(masked, axis=(1, 2))))

def attend_item(items):
    return attend(items[0], items[1], items[2], items[3])

def forward(w_qkv, w_out, w_up, w_down, vector_all, inputs, seg_ids):
    ln1_gain, ln1_shift, q_bias, v_bias, out_bias, ln2_gain, ln2_shift, down_bias, up_bias = split_vectors(vector_all)
    normed = low(layer_norm(inputs, ln1_gain, ln1_shift))
    projected = jnp.dot(normed, w_qkv, precision=HIGH, preferred_element_type=jnp.float32)
    queries = low(low_back(projected[..., :D] + q_bias))
    keys = low(low_back(projected[..., D:2 * D]))
    values = low(low_back(projected[..., 2 * D:] + v_bias))
    mixed, tops = lax.map(jax.checkpoint(attend_item), (queries, keys, values, seg_ids))
    mixed = low(low_back(mixed))
    attended = low_back(jnp.dot(mixed, w_out, precision=HIGH, preferred_element_type=jnp.float32) + out_bias)
    hidden_one = inputs + attended
    normed_two = low(layer_norm(hidden_one, ln2_gain, ln2_shift))
    upper = low_back(jnp.dot(normed_two, w_up, precision=HIGH, preferred_element_type=jnp.float32) + up_bias)
    activated = low(jax.nn.gelu(upper, approximate=False))
    branch = low_back(jnp.dot(activated, w_down, precision=HIGH, preferred_element_type=jnp.float32) + down_bias)
    return (hidden_one + branch, lax.optimization_barrier(jnp.max(tops, axis=0)))

def reference(tokens, segments, out_grad, owners, blocks, first_moment, second_moment, left_bases, right_bases, vectors, vector_first, vector_second):
    slot_of_block, block_at_slot = slot_tables(owners, BPD)
    weights_low = blocks.astype(jnp.bfloat16).astype(jnp.float32)
    matrices = split_blocks(weights_low[slot_of_block])
    vector_low = vectors.astype(jnp.bfloat16).astype(jnp.float32)
    group_size = math.gcd(SEQS, 4)
    groups = SEQS // group_size
    token_groups = tokens.reshape(groups, group_size, LEN, D)
    seg_groups = segments.reshape(groups, group_size, LEN)
    cot_groups = out_grad.reshape(groups, group_size, LEN, D)

    def one_group(carry, items):
        inputs = items[0].astype(jnp.float32)

        def run(w_qkv, w_out, w_up, w_down, vector_all, layer_in):
            return forward(w_qkv, w_out, w_up, w_down, vector_all, layer_in, items[1])
        result, pullback, tops = jax.vjp(run, matrices[0], matrices[1], matrices[2], matrices[3], vector_low, inputs, has_aux=True)
        grads = pullback(items[2].astype(jnp.float32))
        new_carry = tuple((carry[index_one] + grads[index_one] for index_one in range(5)))
        return (new_carry, (result.astype(jnp.bfloat16), grads[5], tops))
    start_carry = tuple((jnp.zeros_like(matrix) for matrix in matrices)) + (jnp.zeros_like(vector_low),)
    summed, (results, input_grads, tops) = lax.scan(one_group, start_carry, (token_groups, seg_groups, cot_groups))
    out_tokens = results.reshape(SEQS, LEN, D)
    input_grad = input_grads.reshape(SEQS, LEN, D)
    grads_by_id = jnp.concatenate([from_matrix(summed[0]), from_matrix(summed[1]), from_matrix(summed[2]), from_matrix(summed[3])], axis=0)
    block_grads = grads_by_id[block_at_slot]
    vector_grads = summed[4]
    grad_norm = jnp.sqrt(jnp.sum(block_grads * block_grads) + jnp.sum(vector_grads * vector_grads))
    clip_factor = jnp.minimum(1.0, math.sqrt(NBLK * BR * BC + VEC) / (grad_norm + 1e-06))
    clipped = block_grads * clip_factor
    new_first = 0.5 * first_moment + 0.5 * clipped
    rotated_grad = rotate_in(clipped, left_bases, right_bases)
    rotated_first = rotate_in(new_first, left_bases, right_bases)
    new_second = 0.5 * second_moment + 0.5 * rotated_grad * rotated_grad
    step_back = rotate_out(rotated_first / (jnp.sqrt(new_second) + 1e-08), left_bases, right_bases)
    updated = blocks - 0.01 * step_back
    vclipped = vector_grads * clip_factor
    new_vector_first = 0.5 * vector_first + 0.5 * vclipped
    new_vector_second = 0.5 * vector_second + 0.5 * vclipped * vclipped
    vupdated = vectors - 0.1 * new_vector_first / (jnp.sqrt(new_vector_second) + 1e-08)
    head_max = lax.optimization_barrier(jnp.max(tops, axis=0))
    tau_value = jnp.mean(head_max)
    clip_factors = tau_value / jnp.maximum(head_max, tau_value)
    root_factor = jnp.sqrt(clip_factors)
    new_blocks = updated * column_scale(block_at_slot, root_factor)[:, None, :]
    new_vectors = vupdated * vector_scale(jnp.arange(VEC, dtype=jnp.int32), root_factor)
    return (out_tokens, input_grad, block_grads, vector_grads, new_blocks, new_first, new_second, new_blocks.astype(jnp.bfloat16), new_vectors, new_vector_first, new_vector_second, new_vectors.astype(jnp.bfloat16), grad_norm, clip_factors)
```

```python
import math

import jax
import jax.numpy as jnp
from jax import lax
from jax.experimental import pallas as pl
from jax.experimental.pallas import tpu as pltpu
from jax.sharding import Mesh
from jax.sharding import PartitionSpec as P

D = 2048
HEADS = 16
DH = 128
FF = 8192
BR = 256
BC = 512
TP = 8
LEN = 1024
CH = 256

F32 = jnp.float32
BF16 = jnp.bfloat16
NEG = -1e30
SCALE = DH ** (-0.5)

EVERY = ("o", "i", "c", "h", "l")
GROUP = ("i", "c", "l")


def at(array, index, axis=0):
    return lax.dynamic_index_in_dim(array, index, axis, keepdims=False)


def trade(array, axis):
    return lax.ppermute(array, axis, [(0, 1), (1, 0)])


def swap_tokens(array):
    return lax.ppermute(array, ("c", "h"), [(0, 0), (1, 2), (2, 1), (3, 3)])


def gather_axis(array, axis, size):
    if size == 1:
        return array[None]
    if size != 2:
        return lax.all_gather(array, axis, axis=0)
    other = trade(array, axis)
    mine = lax.axis_index(axis) == 0
    return jnp.stack([jnp.where(mine, array, other), jnp.where(mine, other, array)])


def scatter_axis(array, axis, size):
    if size == 1:
        return array[0]
    if size != 2:
        return lax.psum_scatter(array, axis, scatter_dimension=0, tiled=False)
    me = lax.axis_index(axis)
    other = trade(at(array, 1 - me), axis)
    return (at(array, me).astype(F32) + other.astype(F32)).astype(BF16)


def over_all(value, combine, collective, outer):
    for axis in ("l", "h", "c", "i"):
        value = combine(value, trade(value, axis))
    if outer == 1:
        return value
    if outer == 2:
        return combine(value, trade(value, "o"))
    return collective(value, "o")


def group_gather(array):
    return lax.all_gather(array, GROUP, axis=0, tiled=True)


def group_scatter(partial):
    i, c, l = (lax.axis_index(name) for name in GROUP)
    x = partial.reshape(2, 2, 2, CH, D)
    other = trade(at(x, 1 - c, 1), "c")
    y = (at(x, c, 1).astype(F32) + other.astype(F32)).astype(BF16)
    first, second = y[..., : D // 2], y[..., D // 2 :]
    first_other = trade(at(first, 1 - i, 0), "i")
    second_other = trade(at(second, 1 - l, 1), "l")
    first = (at(first, i, 0).astype(F32) + first_other.astype(F32)).astype(BF16)
    second = (at(second, l, 1).astype(F32) + second_other.astype(F32)).astype(BF16)
    first_other = trade(at(first, 1 - l), "l")
    second_other = trade(at(second, 1 - i), "i")
    first = at(first, l).astype(F32) + first_other.astype(F32)
    second = at(second, i).astype(F32) + second_other.astype(F32)
    return jnp.concatenate([first, second], axis=1)


def norm_parts(hidden):
    average = jnp.mean(hidden, axis=-1, keepdims=True)
    centred = hidden - average
    variance = jnp.mean(centred * centred, axis=-1, keepdims=True)
    inverse = lax.rsqrt(variance + 1e-05)
    return centred * inverse, inverse


def norm_back(grad, unit, inverse, gain):
    scaled = grad * gain
    inner = jnp.mean(scaled * unit, axis=-1, keepdims=True)
    back = inverse * (scaled - jnp.mean(scaled, axis=-1, keepdims=True) - unit * inner)
    return back, jnp.sum(grad * unit, axis=0), jnp.sum(grad, axis=0)


def contract(left, right, left_dim, right_dim):
    return lax.dot_general(
        left, right, (((left_dim,), (right_dim,)), ((), ())), preferred_element_type=F32
    )


def allowed_pairs(seg_col, seg_row, j, low, high):
    rows = j * CH + lax.broadcasted_iota(jnp.int32, (CH, high - low), 0)
    cols = low + lax.broadcasted_iota(jnp.int32, (CH, high - low), 1)
    same = seg_col[0, j * CH : (j + 1) * CH, :] == seg_row[0, :, low:high]
    return same & (cols <= rows)


def attend_kernel(seg_col, seg_row, q_ref, k_ref, v_ref, o_ref, lse_ref, top_ref):
    top = jnp.full((1, 1), NEG, F32)
    for j in range(LEN // CH):
        low, high = max(0, j - 2) * CH, (j + 1) * CH
        scores = contract(q_ref[j * CH : high, :], k_ref[low:high, :], 1, 1) * SCALE
        scores = jnp.where(allowed_pairs(seg_col, seg_row, j, low, high), scores, NEG)
        peak = jnp.max(scores, axis=-1, keepdims=True)
        weights = jnp.exp(scores - peak)
        total = jnp.sum(weights, axis=-1, keepdims=True)
        probs = (weights * (1.0 / total)).astype(BF16)
        o_ref[j * CH : high, :] = contract(probs, v_ref[low:high, :], 1, 0).astype(BF16)
        lse_ref[0, j * CH : high, :] = peak + jnp.log(total)
        top = jnp.maximum(top, jnp.max(peak, axis=0, keepdims=True))
    top_ref[0] = jnp.broadcast_to(top, (8, 128))


def attend_back_kernel(
    seg_col, seg_row, q_ref, k_ref, v_ref, do_ref, lse_ref, dq_ref, dk_ref, dv_ref, dk_sum, dv_sum
):
    dk_sum[...] = jnp.zeros_like(dk_sum)
    dv_sum[...] = jnp.zeros_like(dv_sum)
    for j in range(LEN // CH):
        low, high = max(0, j - 2) * CH, (j + 1) * CH
        query, keys = q_ref[j * CH : high, :], k_ref[low:high, :]
        grad = do_ref[j * CH : high, :]
        scores = contract(query, keys, 1, 1) * SCALE
        allowed = allowed_pairs(seg_col, seg_row, j, low, high)
        probs = jnp.where(allowed, jnp.exp(scores - lse_ref[0, j * CH : high, :]), 0.0)
        grad_probs = contract(grad, v_ref[low:high, :], 1, 1)
        inner = jnp.sum(probs * grad_probs, axis=-1, keepdims=True)
        grad_scores = (probs * (grad_probs - inner)).astype(BF16)
        dq_ref[j * CH : high, :] = (contract(grad_scores, keys, 1, 0) * SCALE).astype(BF16)
        dk_sum[low:high, :] += contract(grad_scores, query, 0, 0)
        dv_sum[low:high, :] += contract(probs.astype(BF16), grad, 0, 0)
    dk_ref[...] = (dk_sum[...] * SCALE).astype(BF16)
    dv_ref[...] = dv_sum[...].astype(BF16)


def head_specs():
    seg_col = pl.BlockSpec((1, LEN, 1), lambda s, h: (s, 0, 0))
    seg_row = pl.BlockSpec((1, 1, LEN), lambda s, h: (s, 0, 0))
    thirds = [pl.BlockSpec((LEN, DH), lambda s, h, n=n: (s, 2 * n + h)) for n in range(3)]
    lse = pl.BlockSpec((1, LEN, 1), lambda s, h: (2 * s + h, 0, 0))
    return seg_col, seg_row, thirds, lse


def attend(seg_col, seg_row, qkv):
    seg_c, seg_r, thirds, lse = head_specs()
    return pl.pallas_call(
        attend_kernel,
        name="attend",
        grid=(2, 2),
        in_specs=[seg_c, seg_r, *thirds],
        out_specs=[thirds[0], lse, pl.BlockSpec((1, 8, 128), lambda s, h: (2 * s + h, 0, 0))],
        out_shape=[
            jax.ShapeDtypeStruct((2 * LEN, 2 * DH), BF16),
            jax.ShapeDtypeStruct((4, LEN, 1), F32),
            jax.ShapeDtypeStruct((4, 8, 128), F32),
        ],
        compiler_params=pltpu.CompilerParams(vmem_limit_bytes=40 << 20),
        cost_estimate=pl.CostEstimate(flops=1 << 31, bytes_accessed=6 << 20, transcendentals=1 << 22),
    )(seg_col, seg_row, qkv, qkv, qkv)


def attend_back(seg_col, seg_row, qkv, grad, lse_all):
    seg_c, seg_r, thirds, lse = head_specs()
    return pl.pallas_call(
        attend_back_kernel,
        name="attend_back",
        grid=(2, 2),
        in_specs=[seg_c, seg_r, *thirds, thirds[0], lse],
        out_specs=[thirds[0]] * 3,
        out_shape=[jax.ShapeDtypeStruct((2 * LEN, 2 * DH), BF16)] * 3,
        scratch_shapes=[pltpu.VMEM((LEN, DH), F32), pltpu.VMEM((LEN, DH), F32)],
        compiler_params=pltpu.CompilerParams(vmem_limit_bytes=40 << 20),
        cost_estimate=pl.CostEstimate(flops=5 << 30, bytes_accessed=8 << 20, transcendentals=1 << 22),
    )(seg_col, seg_row, qkv, qkv, qkv, grad, lse_all)


def block_tables(owners, per_owner, rank):
    ids = jnp.arange(owners.shape[0], dtype=jnp.int32)
    earlier = (owners[None, :] == owners[:, None]) & (ids[None, :] < ids[:, None])
    slots = owners * per_owner + jnp.sum(earlier.astype(jnp.int32), axis=1)
    mine = rank * per_owner + jnp.arange(per_owner, dtype=jnp.int32)
    own_ids = jnp.sum(jnp.where(slots[None, :] == mine[:, None], ids[None, :], 0), axis=1)
    return slots, own_ids


def column_scale(block_ids, root_factor):
    per_row = 3 * D // BC
    columns = (block_ids % per_row)[:, None] * BC + jnp.arange(BC, dtype=jnp.int32)[None, :]
    head_of = columns % D // DH
    picked = jnp.sum(
        jnp.where(head_of[..., None] == jnp.arange(HEADS, dtype=jnp.int32), root_factor, 0.0), axis=-1
    )
    inside = (block_ids < D // BR * per_row)[:, None] & (columns < 2 * D)
    return jnp.where(inside, picked, 1.0)


def vector_scale(positions, root_factor):
    inside = (positions < 8 * D) & (positions % 8 == 2)
    head_of = positions // 8 // DH
    picked = jnp.sum(
        jnp.where(head_of[:, None] == jnp.arange(HEADS, dtype=jnp.int32), root_factor, 0.0), axis=-1
    )
    return jnp.where(inside, picked, 1.0)


def rotate(left, matrix, right, left_dim, right_dim):
    done = lax.dot_general(
        left, matrix, (((left_dim,), (1,)), ((0,), (0,))),
        precision=lax.Precision.HIGH, preferred_element_type=F32,
    )
    return lax.dot_general(
        done, right, (((2,), (right_dim,)), ((0,), (0,))),
        precision=lax.Precision.HIGH, preferred_element_type=F32,
    )


def make_local(outer):
    devices = outer * 16
    rows = BR // devices
    qkv_end = D // BR * (3 * D // BC)
    out_end = qkv_end + D // BR * (D // BC)
    up_end = out_end + D // BR * (FF // BC)

    def pieces_to_group(pieces):
        got = lax.all_to_all(pieces, GROUP, 0, 0, tiled=True)
        return gather_axis(gather_axis(got, "h", 2), "o", outer)

    def piece_major(full, unit_shape):
        return full.reshape(outer, 2, 2, 2, 2, *unit_shape)

    def in_qkv(full):
        full = piece_major(full, (8, 3, rows, CH))
        return full.transpose(5, 0, 2, 3, 1, 4, 7, 6, 8).reshape(D, 3 * CH)

    def in_out(full):
        full = piece_major(full, (4, rows, BC))
        return full.transpose(0, 2, 3, 1, 4, 6, 5, 7).reshape(CH, D)

    def in_up(full):
        full = piece_major(full, (8, 2, rows, BC))
        return full.transpose(5, 0, 2, 3, 1, 4, 7, 6, 8).reshape(D, FF // TP)

    def in_down(full):
        full = piece_major(full, (4, 4, rows, BC))
        return full.transpose(5, 0, 2, 3, 1, 4, 7, 6, 8).reshape(FF // TP, D)

    def reduce_pieces(full):
        part = scatter_axis(scatter_axis(full, "o", outer), "h", 2)
        return lax.all_to_all(part, GROUP, 0, 0, tiled=True)

    def out_three(grad, row_units, col_units, width):
        full = grad.astype(BF16).reshape(row_units, outer, 2, 2, 2, 2, rows, col_units, width)
        full = full.transpose(1, 4, 2, 3, 5, 0, 7, 6, 8)
        return full.reshape(outer, 2, TP * row_units * col_units, rows, width)

    def local(
        tokens, segments, out_grad, owners, blocks, first_moment, second_moment,
        left_bases, right_bases, vectors, vector_first, vector_second,
    ):
        per_owner, vector_part = blocks.shape[0], vectors.shape[0]
        o, i, c, h, l = (lax.axis_index(name) for name in EVERY)
        rank = (((o * 2 + i) * 2 + c) * 2 + h) * 2 + l
        member = (i * 2 + c) * 2 + l
        slots, own_ids = block_tables(owners, per_owner, rank)

        order = jnp.concatenate(
            [
                slots[:qkv_end].reshape(8, 3, 4).transpose(2, 0, 1).reshape(-1),
                slots[qkv_end:out_end],
                slots[out_end:up_end].reshape(8, 8, 2).transpose(1, 0, 2).reshape(-1),
                slots[up_end:],
            ]
        )
        pick = (order[:, None] == jnp.arange(order.shape[0], dtype=jnp.int32)[None, :]).astype(BF16)
        sent = blocks.astype(BF16).reshape(per_owner, devices, rows, BC).transpose(1, 0, 2, 3)
        pieces = lax.all_to_all(sent.reshape(-1, rows, BC), EVERY, 0, 0, tiled=True)
        pieces = lax.dot_general(pick, pieces, (((1,), (0,)), ((), ())), preferred_element_type=BF16)
        part_qkv = (
            pieces[:qkv_end].reshape(4, 24, rows, 2, CH).transpose(0, 3, 1, 2, 4).reshape(-1, rows, CH)
        )
        w_qkv = in_qkv(pieces_to_group(part_qkv))
        w_out = in_out(pieces_to_group(pieces[qkv_end:out_end]))
        w_up = in_up(pieces_to_group(pieces[out_end:up_end]))
        w_down = in_down(pieces_to_group(pieces[up_end:]))

        vector_all = vectors.astype(BF16)
        for axis in ("l", "h", "c", "i"):
            vector_all = gather_axis(vector_all, axis, 2).reshape(-1)
        vector_all = gather_axis(vector_all, "o", outer).reshape(-1).astype(F32)
        feature = vector_all[: 8 * D].reshape(D, 8)
        ln1_gain, ln1_shift, q_bias, v_bias, out_bias, ln2_gain, ln2_shift, down_bias = (
            feature[:, n] for n in range(8)
        )
        up_bias = lax.dynamic_slice_in_dim(vector_all, 8 * D + member * (FF // TP), FF // TP)
        qkv_bias = jnp.concatenate(
            [
                lax.dynamic_slice_in_dim(q_bias, member * CH, CH),
                jnp.zeros((CH,), F32),
                lax.dynamic_slice_in_dim(v_bias, member * CH, CH),
            ]
        )

        x = swap_tokens(tokens.reshape(CH, D)).astype(F32)
        dy = swap_tokens(out_grad.reshape(CH, D))
        dy_all = group_gather(dy)
        seg = jnp.where(c == h, segments, trade(segments, "c"))
        seg = gather_axis(seg, "i", 2).reshape(2, LEN)
        seg_col, seg_row = seg[:, :, None], seg[:, None, :]
        unit1, inverse1 = norm_parts(x)
        a_all = group_gather((unit1 * ln1_gain + ln1_shift).astype(BF16))
        qkv = (jnp.dot(a_all, w_qkv, preferred_element_type=F32) + qkv_bias).astype(BF16)
        mixed, lse, tops = attend(seg_col, seg_row, qkv)
        attended = group_scatter(jnp.dot(mixed, w_out, preferred_element_type=F32).astype(BF16))
        h1 = x + attended + out_bias
        unit2, inverse2 = norm_parts(h1)
        c_all = group_gather((unit2 * ln2_gain + ln2_shift).astype(BF16))
        u = jnp.dot(c_all, w_up, preferred_element_type=F32) + up_bias
        cdf = 0.5 * (1.0 + lax.erf(u * math.sqrt(0.5)))
        g = (u * cdf).astype(BF16)
        branch = group_scatter(jnp.dot(g, w_down, preferred_element_type=F32).astype(BF16))
        out_tokens = swap_tokens((h1 + branch + down_bias).astype(BF16))

        dg = contract(dy_all, w_down, 1, 1)
        slope = cdf + u * jnp.exp(-0.5 * u * u) * (1.0 / math.sqrt(2.0 * math.pi))
        du = (dg * slope).astype(BF16)
        dc = group_scatter(contract(du, w_up, 1, 1).astype(BF16))
        back2, ln2_gain_grad, ln2_shift_grad = norm_back(dc, unit2, inverse2, ln2_gain)
        dh1 = dy.astype(F32) + back2
        da_own = dh1.astype(BF16)
        da_all = group_gather(da_own)
        do = contract(da_all, w_out, 1, 1).astype(BF16)
        dqkv = jnp.concatenate(attend_back(seg_col, seg_row, qkv, do, lse), axis=1)
        da = group_scatter(contract(dqkv, w_qkv, 1, 1).astype(BF16))
        back1, ln1_gain_grad, ln1_shift_grad = norm_back(da, unit1, inverse1, ln1_gain)
        input_grad = swap_tokens((dh1 + back1).astype(BF16)).astype(F32)

        got_down = reduce_pieces(out_three(contract(g, dy_all, 0, 0), 4, 4, BC))
        got_up = reduce_pieces(out_three(contract(c_all, du, 0, 0), 8, 2, BC))
        got_out = reduce_pieces(out_three(contract(mixed, da_all, 0, 0), 1, 4, BC))
        got_qkv = reduce_pieces(out_three(contract(a_all, dqkv, 0, 0), 8, 3, CH))
        got_qkv = got_qkv.reshape(4, 2, 24, rows, CH).transpose(0, 2, 3, 1, 4).reshape(-1, rows, BC)
        got = jnp.concatenate([got_qkv, got_out, got_up, got_down], axis=0)
        got = lax.dot_general(pick, got, (((0,), (0,)), ((), ())), preferred_element_type=BF16)
        got = lax.all_to_all(got, EVERY, 0, 0, tiled=True)
        block_grads = (
            got.reshape(devices, per_owner, rows, BC).transpose(1, 0, 2, 3)
            .reshape(per_owner, BR, BC).astype(F32)
        )

        dqkv_sum = jnp.sum(dqkv.astype(F32), axis=0)

        def spread(values, size):
            return lax.dynamic_update_slice_in_dim(jnp.zeros((size,), F32), values, member * values.shape[0], 0)

        terms = jnp.stack(
            [
                ln1_gain_grad, ln1_shift_grad, spread(dqkv_sum[:CH], D), spread(dqkv_sum[2 * CH :], D),
                jnp.sum(da_own.astype(F32), axis=0), ln2_gain_grad, ln2_shift_grad,
                jnp.sum(dy.astype(F32), axis=0),
            ],
            axis=1,
        ).reshape(-1)
        terms = jnp.concatenate([terms, spread(jnp.sum(du.astype(F32), axis=0), FF)])
        terms = lax.all_to_all(terms.reshape(devices, vector_part), EVERY, 0, 0, tiled=True)
        vector_grads = jnp.sum(terms, axis=0)

        square = jnp.sum(block_grads * block_grads) + jnp.sum(vector_grads * vector_grads)
        grad_norm = jnp.sqrt(over_all(square, jnp.add, lax.psum, outer))
        total_params = slots.shape[0] * BR * BC + vector_part * devices
        clip = jnp.minimum(1.0, math.sqrt(total_params) / (grad_norm + 1e-06))
        turned_first = rotate(left_bases, first_moment, right_bases, 1, 1)
        turned_grad = rotate(left_bases, block_grads, right_bases, 1, 1)
        new_first = 0.5 * first_moment + (0.5 * clip) * block_grads
        new_second = 0.5 * second_moment + 0.5 * jnp.square(clip * turned_grad)
        ratio = (0.5 * turned_first + (0.5 * clip) * turned_grad) / (jnp.sqrt(new_second) + 1e-08)
        updated = blocks - 0.01 * rotate(left_bases, ratio, right_bases, 2, 2)
        vclipped = vector_grads * clip
        new_vector_first = 0.5 * vector_first + 0.5 * vclipped
        new_vector_second = 0.5 * vector_second + 0.5 * vclipped * vclipped
        vupdated = vectors - 0.1 * new_vector_first / (jnp.sqrt(new_vector_second) + 1e-08)
        head_ids = jnp.arange(HEADS, dtype=jnp.int32)
        tops = jnp.max(tops[:, 0, 0].reshape(2, 2), axis=0)
        tops = jnp.where(head_ids // 2 == member, jnp.where(head_ids % 2 == 0, tops[0], tops[1]), NEG)
        head_max = over_all(tops, jnp.maximum, lax.pmax, outer)
        tau = jnp.mean(head_max)
        clip_factors = tau / jnp.maximum(head_max, tau)
        root_factor = jnp.sqrt(clip_factors)
        new_blocks = updated * column_scale(own_ids, root_factor)[:, None, :]
        positions = rank * vector_part + jnp.arange(vector_part, dtype=jnp.int32)
        new_vectors = vupdated * vector_scale(positions, root_factor)
        return (
            out_tokens[None],
            input_grad[None],
            block_grads,
            vector_grads,
            new_blocks,
            new_first,
            new_second,
            new_blocks.astype(BF16),
            new_vectors,
            new_vector_first,
            new_vector_second,
            new_vectors.astype(BF16),
            grad_norm,
            clip_factors,
        )

    return local


def solution(mesh):
    outer = mesh.shape["dp"] // 4
    fine = Mesh(mesh.devices.reshape(outer, 2, 2, 2, 2), EVERY)
    seq, pos = ("o", "i", "c"), ("h", "l")
    token, owned, entry = P(seq, pos, None), P(EVERY, None, None), P(EVERY)
    return jax.shard_map(
        make_local(outer),
        mesh=fine,
        in_specs=(token, P(seq, None), token, P(), *[owned] * 5, *[entry] * 3),
        out_specs=(token, token, owned, entry, *[owned] * 4, *[entry] * 4, P(), P()),
        check_vma=False,
    )
```

```python
import functools
import math

import jax
import jax.numpy as jnp
from jax import lax
from jax.experimental import pallas as pl
from jax.experimental.pallas import tpu as pltpu
from jax.sharding import Mesh
from jax.sharding import PartitionSpec as P

D = 2048
HEADS = 16
DH = 128
FF = 8192
BR = 256
BC = 512
TP = 8
LEN = 1024
CH = 256

F32 = jnp.float32
BF16 = jnp.bfloat16
NEG = -1e30
SCALE = DH ** (-0.5)

EVERY = ("p", "q", "i", "c", "h", "l")
GROUP = ("q", "i", "c")
DATA = ("p", "h", "l")


def at(array, index, axis=0):
    return lax.dynamic_index_in_dim(array, index, axis, keepdims=False)


def trade(array, axis):
    return lax.ppermute(array, axis, [(0, 1), (1, 0)])


def after(value, *others):
    return lax.optimization_barrier((value, others))[0]


def together(*values):
    return lax.optimization_barrier(values)


def nothing_of(array):
    return array[(0,) * array.ndim].astype(F32) * 0.0


def swap_tokens(array):
    bits = [(i, c, h, l) for i in range(2) for c in range(2) for h in range(2) for l in range(2)]
    pairs = [(8 * i + 4 * c + 2 * h + l, 8 * l + 4 * h + 2 * c + i) for i, c, h, l in bits]
    other = lax.ppermute(array, ("i", "c", "h", "l"), [pair for pair in pairs if pair[0] != pair[1]])
    i, c, h, l = (lax.axis_index(name) for name in ("i", "c", "h", "l"))
    return jnp.where((i == l) & (c == h), array, other)


def pair_up(array, axis):
    other = trade(array, axis)
    mine = lax.axis_index(axis) == 0
    return jnp.stack([jnp.where(mine, array, other), jnp.where(mine, other, array)])


def group_gather(array):
    return lax.all_gather(array, GROUP, axis=0, tiled=True)


def to_relative(array):
    q, i, c = (lax.axis_index(name) for name in GROUP)
    rows = [at(at(at(array, q ^ m, 0), c ^ n, 0), i ^ k, 0) for n in range(2) for m in range(2) for k in range(2)]
    return jnp.stack(rows).reshape(2, 2, 2, *array.shape[3:])


def to_member(array):
    q, i, c = (lax.axis_index(name) for name in GROUP)
    rows = [at(at(at(array, c ^ n, 0), q ^ m, 0), i ^ k, 0) for m in range(2) for n in range(2) for k in range(2)]
    return jnp.stack(rows).reshape(2, 2, 2, *array.shape[3:])


def gather_relative(own, *fillers):
    first, second = own[:, : D // 2], own[:, D // 2 :]
    first = jnp.stack([first, trade(first, "i")])
    second = jnp.stack([second, trade(second, "q")])
    first_other, second_other = trade(first, "q"), trade(second, "i")
    zero = sum((nothing_of(filler) for filler in fillers), jnp.float32(0)).astype(BF16)
    first = jnp.stack([first, first_other + zero])
    second = jnp.stack([second, second_other + zero]).transpose(1, 0, 2, 3)
    mine = jnp.concatenate([first, second], axis=-1).reshape(4 * CH, D)
    return mine, trade(mine, "c")


def scatter_relative(pair, *fillers):
    total = (pair[0] + pair[1].astype(F32)).astype(BF16).reshape(2, 2, CH, D)
    first, second = total[..., : D // 2], total[..., D // 2 :]
    first_other = trade(first[1], "q")
    second_other = trade(second[:, 1], "i")
    zero = sum((nothing_of(filler) for filler in fillers), jnp.float32(0))
    first = (first[0].astype(F32) + (first_other.astype(F32) + zero)).astype(BF16)
    second = (second[:, 0].astype(F32) + (second_other.astype(F32) + zero)).astype(BF16)
    first_other = trade(first[1], "i")
    second_other = trade(second[1], "q")
    return jnp.concatenate(
        [first[0].astype(F32) + first_other.astype(F32), second[0].astype(F32) + second_other.astype(F32)], axis=1
    )


def scatter_core(left, right, right_dim):
    c = lax.axis_index("c")
    left = left.reshape(2, 2, 2 * CH, -1)
    send = contract(at(left, 1 - c, 1).reshape(4 * CH, -1), right, 1, right_dim).astype(BF16)
    keep = contract(at(left, c, 1).reshape(4 * CH, -1), right, 1, right_dim)
    return keep, trade(send, "c")


def scatter_chips(pair):
    q, i = lax.axis_index("q"), lax.axis_index("i")
    total = (pair[0] + pair[1].astype(F32)).astype(BF16).reshape(2, 2, CH, D)
    first, second = total[..., : D // 2], total[..., D // 2 :]
    first_other = trade(at(first, 1 - q, 0), "q")
    second_other = trade(at(second, 1 - i, 1), "i")
    first = (at(first, q, 0).astype(F32) + first_other.astype(F32)).astype(BF16)
    second = (at(second, i, 1).astype(F32) + second_other.astype(F32)).astype(BF16)
    first_other = trade(at(first, 1 - i), "i")
    second_other = trade(at(second, 1 - q), "q")
    first = at(first, i).astype(F32) + first_other.astype(F32)
    second = at(second, q).astype(F32) + second_other.astype(F32)
    return jnp.concatenate([first, second], axis=1)


def norm_parts(hidden):
    average = jnp.mean(hidden, axis=-1, keepdims=True)
    centred = hidden - average
    variance = jnp.mean(centred * centred, axis=-1, keepdims=True)
    inverse = lax.rsqrt(variance + 1e-05)
    return centred * inverse, inverse


def norm_back(grad, unit, inverse, gain):
    scaled = grad * gain
    inner = jnp.mean(scaled * unit, axis=-1, keepdims=True)
    back = inverse * (scaled - jnp.mean(scaled, axis=-1, keepdims=True) - unit * inner)
    return back, jnp.sum(grad * unit, axis=0), jnp.sum(grad, axis=0)


def contract(left, right, left_dim, right_dim):
    return lax.dot_general(
        left, right, (((left_dim,), (right_dim,)), ((), ())), preferred_element_type=F32
    )


def allowed_pairs(seg_col, seg_row, j, low, high):
    rows = j * CH + lax.broadcasted_iota(jnp.int32, (CH, high - low), 0)
    cols = low + lax.broadcasted_iota(jnp.int32, (CH, high - low), 1)
    same = seg_col[0, j * CH : (j + 1) * CH, :] == seg_row[0, :, low:high]
    return same & (cols <= rows)


def attend_kernel(seg_col, seg_row, q_ref, k_ref, v_ref, o_ref, lse_ref, top_ref):
    top = jnp.full((1, 1), NEG, F32)
    for j in range(LEN // CH):
        low, high = max(0, j - 2) * CH, (j + 1) * CH
        scores = contract(q_ref[j * CH : high, :], k_ref[low:high, :], 1, 1) * SCALE
        scores = jnp.where(allowed_pairs(seg_col, seg_row, j, low, high), scores, NEG)
        peak = jnp.max(scores, axis=-1, keepdims=True)
        weights = jnp.exp(scores - peak)
        total = jnp.sum(weights, axis=-1, keepdims=True)
        probs = (weights * (1.0 / total)).astype(BF16)
        o_ref[j * CH : high, :] = contract(probs, v_ref[low:high, :], 1, 0).astype(BF16)
        lse_ref[0, j * CH : high, :] = peak + jnp.log(total)
        top = jnp.maximum(top, jnp.max(peak, axis=0, keepdims=True))
    top_ref[0] = jnp.broadcast_to(top, (8, 128))


def attend_back_kernel(
    seg_col, seg_row, q_ref, k_ref, v_ref, do_ref, lse_ref, dq_ref, dk_ref, dv_ref, dk_sum, dv_sum
):
    dk_sum[...] = jnp.zeros_like(dk_sum)
    dv_sum[...] = jnp.zeros_like(dv_sum)
    for j in range(LEN // CH):
        low, high = max(0, j - 2) * CH, (j + 1) * CH
        query, keys = q_ref[j * CH : high, :], k_ref[low:high, :]
        grad = do_ref[j * CH : high, :]
        scores = contract(query, keys, 1, 1) * SCALE
        allowed = allowed_pairs(seg_col, seg_row, j, low, high)
        probs = jnp.where(allowed, jnp.exp(scores - lse_ref[0, j * CH : high, :]), 0.0)
        grad_probs = contract(grad, v_ref[low:high, :], 1, 1)
        inner = jnp.sum(probs * grad_probs, axis=-1, keepdims=True)
        grad_scores = (probs * (grad_probs - inner)).astype(BF16)
        dq_ref[j * CH : high, :] = (contract(grad_scores, keys, 1, 0) * SCALE).astype(BF16)
        dk_sum[low:high, :] += contract(grad_scores, query, 0, 0)
        dv_sum[low:high, :] += contract(probs.astype(BF16), grad, 0, 0)
    dk_ref[...] = (dk_sum[...] * SCALE).astype(BF16)
    dv_ref[...] = dv_sum[...].astype(BF16)


def head_specs():
    seg_col = pl.BlockSpec((1, LEN, 1), lambda s, h: (s, 0, 0))
    seg_row = pl.BlockSpec((1, 1, LEN), lambda s, h: (s, 0, 0))
    thirds = [pl.BlockSpec((LEN, DH), lambda s, h, n=n: (s, 2 * n + h)) for n in range(3)]
    lse = pl.BlockSpec((1, LEN, 1), lambda s, h: (2 * s + h, 0, 0))
    return seg_col, seg_row, thirds, lse


def attend(seg_col, seg_row, qkv):
    seg_c, seg_r, thirds, lse = head_specs()
    return pl.pallas_call(
        attend_kernel,
        name="attend",
        grid=(2, 2),
        in_specs=[seg_c, seg_r, *thirds],
        out_specs=[thirds[0], lse, pl.BlockSpec((1, 8, 128), lambda s, h: (2 * s + h, 0, 0))],
        out_shape=[
            jax.ShapeDtypeStruct((2 * LEN, 2 * DH), BF16),
            jax.ShapeDtypeStruct((4, LEN, 1), F32),
            jax.ShapeDtypeStruct((4, 8, 128), F32),
        ],
        compiler_params=pltpu.CompilerParams(vmem_limit_bytes=40 << 20),
        cost_estimate=pl.CostEstimate(flops=1 << 20, bytes_accessed=1 << 10, transcendentals=0),
    )(seg_col, seg_row, qkv, qkv, qkv)


def attend_back(seg_col, seg_row, qkv, grad, lse_all):
    seg_c, seg_r, thirds, lse = head_specs()
    return pl.pallas_call(
        attend_back_kernel,
        name="attend_back",
        grid=(2, 2),
        in_specs=[seg_c, seg_r, *thirds, thirds[0], lse],
        out_specs=[thirds[0]] * 3,
        out_shape=[jax.ShapeDtypeStruct((2 * LEN, 2 * DH), BF16)] * 3,
        scratch_shapes=[pltpu.VMEM((LEN, DH), F32), pltpu.VMEM((LEN, DH), F32)],
        compiler_params=pltpu.CompilerParams(vmem_limit_bytes=40 << 20),
        cost_estimate=pl.CostEstimate(flops=5 << 30, bytes_accessed=8 << 20, transcendentals=1 << 22),
    )(seg_col, seg_row, qkv, qkv, qkv, grad, lse_all)


def lay_out_kernel(fold, in_ref, out_ref):
    parts, _, col_units, rows, width = in_ref.shape
    height, width = parts * rows, width // fold
    for j in range(col_units):
        for k in range(fold):
            piece = in_ref[:, 0, j, :, k * width : (k + 1) * width].reshape(height, width)
            out_ref[k * height : (k + 1) * height, j * width : (j + 1) * width] = piece


def lay_out(full, fold=1):
    parts, row_units, col_units, rows, width = full.shape
    block = (fold * parts * rows, col_units * width // fold)
    shape = (row_units * block[0], block[1])
    return pl.pallas_call(
        functools.partial(lay_out_kernel, fold),
        name="lay_out",
        grid=(row_units,),
        in_specs=[pl.BlockSpec((parts, 1, col_units, rows, width), lambda n: (0, n, 0, 0, 0))],
        out_specs=pl.BlockSpec(block, lambda n: (n, 0)),
        out_shape=jax.ShapeDtypeStruct(shape, BF16),
        compiler_params=pltpu.CompilerParams(vmem_limit_bytes=24 << 20),
        cost_estimate=pl.CostEstimate(flops=0, bytes_accessed=4 * shape[0] * shape[1], transcendentals=0),
    )(full)


def block_tables(owners, per_owner, rank):
    ids = jnp.arange(owners.shape[0], dtype=jnp.int32)
    earlier = (owners[None, :] == owners[:, None]) & (ids[None, :] < ids[:, None])
    slots = owners * per_owner + jnp.sum(earlier.astype(jnp.int32), axis=1)
    mine = rank * per_owner + jnp.arange(per_owner, dtype=jnp.int32)
    own_ids = jnp.sum(jnp.where(slots[None, :] == mine[:, None], ids[None, :], 0), axis=1)
    return slots, own_ids


def column_scale(block_ids, root_factor):
    per_row = 3 * D // BC
    columns = (block_ids % per_row)[:, None] * BC + jnp.arange(BC, dtype=jnp.int32)[None, :]
    head_of = columns % D // DH
    picked = jnp.sum(
        jnp.where(head_of[..., None] == jnp.arange(HEADS, dtype=jnp.int32), root_factor, 0.0), axis=-1
    )
    inside = (block_ids < D // BR * per_row)[:, None] & (columns < 2 * D)
    return jnp.where(inside, picked, 1.0)


def vector_scale(positions, root_factor):
    inside = (positions < 8 * D) & (positions % 8 == 2)
    head_of = positions // 8 // DH
    picked = jnp.sum(
        jnp.where(head_of[:, None] == jnp.arange(HEADS, dtype=jnp.int32), root_factor, 0.0), axis=-1
    )
    return jnp.where(inside, picked, 1.0)


def split3(matrix):
    high = matrix.astype(BF16)
    return high, (matrix - high.astype(F32)).astype(BF16)


def dot3(left, right, right_dim=0):
    (a, b), (c, d) = left, right
    return contract(a, c, 1, right_dim) + (contract(a, d, 1, right_dim) + contract(b, c, 1, right_dim))


def update_kernel(
    clip_ref, scale_ref, grad_ref, first_ref, second_ref, left_ref, right_ref, block_ref,
    new_block_ref, new_first_ref, new_second_ref, copy_ref,
):
    grad = clip_ref[0] * grad_ref[0]
    new_first = 0.5 * first_ref[0] + 0.5 * grad
    new_first_ref[0] = new_first
    left, right = left_ref[0], split3(right_ref[0])
    turned = dot3(split3(left.T), split3(jnp.concatenate([grad, new_first], axis=1)))
    turned = dot3(split3(jnp.concatenate([turned[:, :BC], turned[:, BC:]], axis=0)), right)
    new_second = 0.5 * second_ref[0] + 0.5 * jnp.square(turned[:BR])
    new_second_ref[0] = new_second
    ratio = turned[BR:] / (jnp.sqrt(new_second) + 1e-08)
    back = dot3(split3(dot3(split3(left), split3(ratio))), right, 1)
    new_block = (block_ref[0] - 0.01 * back) * scale_ref[0]
    new_block_ref[0] = new_block
    copy_ref[0] = new_block.astype(BF16)


def update_blocks(clip, scale, grads, first, second, left, right, blocks):
    count = blocks.shape[0]
    one = pl.BlockSpec((1, BR, BC), lambda n: (n, 0, 0))
    whole = jax.ShapeDtypeStruct(blocks.shape, F32)
    return pl.pallas_call(
        update_kernel,
        name="update_blocks",
        grid=(count,),
        in_specs=[
            pl.BlockSpec(memory_space=pltpu.SMEM),
            pl.BlockSpec((1, 1, BC), lambda n: (n, 0, 0)),
            one, one, one,
            pl.BlockSpec((1, BR, BR), lambda n: (n, 0, 0)),
            pl.BlockSpec((1, BC, BC), lambda n: (n, 0, 0)),
            one,
        ],
        out_specs=[one] * 4,
        out_shape=[whole, whole, whole, jax.ShapeDtypeStruct(blocks.shape, BF16)],
        compiler_params=pltpu.CompilerParams(vmem_limit_bytes=40 << 20),
        cost_estimate=pl.CostEstimate(
            flops=count * (18 << 26), bytes_accessed=count * (23 << 18), transcendentals=count << 17
        ),
    )(clip.reshape(1), scale[:, None, :], grads, first, second, left, right, blocks)


def make_local(outer):
    devices = outer * 32
    rows = BR // devices
    qkv_end = D // BR * (3 * D // BC)
    out_end = qkv_end + D // BR * (D // BC)
    up_end = out_end + D // BR * (FF // BC)

    def everyone(array):
        return lax.all_to_all(array, EVERY, 0, 0, tiled=True)

    def grouped(array):
        return lax.all_to_all(array, GROUP, 0, 0, tiled=True)

    def cut(matrices):
        parts = matrices.reshape(matrices.shape[0], outer, 2, 2, 2, 2, 2, rows, BC)
        return parts.transpose(1, 4, 5, 6, 2, 3, 0, 7, 8).reshape(-1, rows, BC)

    def uncut(parts, count):
        parts = parts.reshape(outer, 2, 2, 2, 2, 2, count, rows, BC)
        return parts.transpose(6, 0, 4, 5, 1, 2, 3, 7, 8).reshape(count, BR, BC)

    def assemble(full, row_units, col_units, width):
        full = full.reshape(devices, row_units, col_units, rows, width)
        if rows != 8:
            return full.transpose(1, 0, 3, 2, 4).reshape(row_units * BR, col_units * width)
        return lay_out(full)

    def assemble_qkv(full):
        full = full.reshape(devices, 4, 3, rows, BC)
        if rows != 8:
            full = full.reshape(devices, 4, 3, rows, 2, CH).transpose(1, 4, 0, 3, 2, 5)
            return full.reshape(D, 3 * CH)
        return lay_out(full, 2)

    def take_apart(grad, row_units, col_units, width):
        full = grad.astype(BF16).reshape(row_units, devices, rows, col_units, width)
        full = full.transpose(1, 0, 3, 2, 4)
        return full.reshape(outer * 4, TP, row_units * col_units, rows, width)

    def local(
        tokens, segments, out_grad, owners, blocks, first_moment, second_moment,
        left_bases, right_bases, vectors, vector_first, vector_second,
    ):
        per_owner, vector_part = blocks.shape[0], vectors.shape[0]
        p, q, i, c, h, l = (lax.axis_index(name) for name in EVERY)
        rank = ((((p * 2 + q) * 2 + i) * 2 + c) * 2 + h) * 2 + l
        member = (q * 2 + i) * 2 + c

        def data_gather(piece):
            return lax.all_gather(piece, DATA, axis=0)

        def data_scatter(full):
            return lax.psum_scatter(full, DATA, scatter_dimension=0, tiled=False)

        low = jnp.pad(vectors.astype(BF16), (0, rows * BC - vector_part))
        low = jnp.broadcast_to(low.reshape(1, 1, rows, BC), (devices, 1, rows, BC))
        sent = jnp.concatenate([cut(blocks.astype(BF16)).reshape(devices, per_owner, rows, BC), low], axis=1)
        pieces = everyone(sent.reshape(-1, rows, BC))
        seg = at(at(pair_up(pair_up(segments, "c"), "i"), l), h)
        seg = pair_up(seg, "q").reshape(2, LEN)
        seg_col, seg_row = seg[:, :, None], seg[:, None, :]
        x_low = swap_tokens(tokens.reshape(CH, D))
        dy = swap_tokens(out_grad.reshape(CH, D))
        x_all = group_gather(x_low).reshape(2, 2, 2, CH, D)
        dy_all = group_gather(dy).reshape(2, 2, 2, CH, D)
        slots, own_ids = block_tables(owners, per_owner, rank)
        rest_order = jnp.concatenate(
            [
                slots[qkv_end:out_end].reshape(TP, -1),
                slots[out_end:up_end].reshape(8, TP, 2).transpose(1, 0, 2).reshape(TP, -1),
                slots[up_end:].reshape(TP, -1),
            ],
            axis=1,
        )
        order = jnp.concatenate(
            [slots[:qkv_end].reshape(8, 3, 4).transpose(2, 0, 1).reshape(-1), rest_order.reshape(-1)]
        )
        order = order + order // per_owner + (nothing_of(seg_row) + nothing_of(x_low) + nothing_of(dy)).astype(jnp.int32)
        got_order = order - order // (per_owner + 1)
        place = jnp.arange(devices * (per_owner + 1), dtype=jnp.int32)
        pick = (order[:, None] == place[None, :]).astype(BF16)
        got_pick = (got_order[:, None] == place[None, : devices * per_owner]).astype(BF16)
        vector_all = pieces.reshape(devices, per_owner + 1, rows * BC)[:, per_owner, :vector_part]
        vector_all = vector_all.reshape(-1).astype(F32)
        feature = vector_all[: 8 * D].reshape(D, 8)
        ln1_gain, ln1_shift, q_bias, v_bias, out_bias, ln2_gain, ln2_shift, down_bias = (
            feature[:, n] for n in range(8)
        )
        up_bias = lax.dynamic_slice_in_dim(vector_all, 8 * D + member * (FF // TP), FF // TP)
        qkv_bias = jnp.concatenate(
            [
                lax.dynamic_slice_in_dim(q_bias, member * CH, CH),
                jnp.zeros((CH,), F32),
                lax.dynamic_slice_in_dim(v_bias, member * CH, CH),
            ]
        )
        pieces = lax.dot_general(pick, pieces, (((1,), (0,)), ((), ())), preferred_element_type=BF16)
        part = pieces[:qkv_end].reshape(4, 4, 2, 3, rows, 2, CH).transpose(0, 5, 1, 3, 4, 2, 6)
        part = jnp.concatenate(
            [part.reshape(TP, 12, rows, BC), pieces[qkv_end:].reshape(TP, 36, rows, BC)], axis=1
        )
        part = grouped(part.reshape(-1, rows, BC)).reshape(TP, 48, rows, BC)
        part, x_all = together(part, x_all)
        w_first, part = together(data_gather(part[:, :16]), part)
        w_qkv, w_out = w_first[:, :, :12], w_first[:, :, 12:]
        w_up = data_gather(part[:, 16:32])
        w_down = data_gather(part[:, 32:])
        w_qkv = assemble_qkv(w_qkv)
        w_out = assemble(w_out, 1, 4, BC)
        x = x_low.astype(F32)
        unit_all, _ = norm_parts(x_all.reshape(2 * LEN, D).astype(F32))
        a_all = (unit_all * ln1_gain + ln1_shift).astype(BF16)
        a_all = a_all.reshape(2, 2, 2, CH, D).transpose(0, 2, 1, 3, 4).reshape(2 * LEN, D)
        dy_all = to_relative(dy_all.transpose(0, 2, 1, 3, 4)).reshape(2, 4 * CH, D)
        unit1, inverse1 = norm_parts(x)

        a_all, dy_all = together(a_all, dy_all)
        qkv = (jnp.dot(a_all, w_qkv, preferred_element_type=F32) + qkv_bias).astype(BF16)
        mixed, lse, tops = attend(seg_col, seg_row, qkv)
        h1 = x + scatter_chips(scatter_core(mixed, w_out, 0)) + out_bias
        unit2, inverse2 = norm_parts(h1)
        c_own, w_up = together((unit2 * ln2_gain + ln2_shift).astype(BF16), w_up)
        w_up = assemble(w_up, 8, 2, BC)
        c_two = gather_relative(c_own)

        u_two = [jnp.dot(tokens_of, w_up, preferred_element_type=F32) + up_bias for tokens_of in c_two]
        u_two[0], u_two[1], w_down = together(u_two[0], u_two[1], w_down)
        w_down = assemble(w_down, 4, 4, BC)

        def half(u, grads):
            dg = contract(grads, w_down, 1, 1)
            cdf = 0.5 * (1.0 + lax.erf(u * math.sqrt(0.5)))
            slope = cdf + u * jnp.exp(-0.5 * u * u) * (1.0 / math.sqrt(2.0 * math.pi))
            return (u * cdf).astype(BF16), (dg * slope).astype(BF16)

        g_mine, du_mine = half(u_two[0], dy_all[0])
        g_other, du_other = half(u_two[1], dy_all[1])
        grad_down = contract(g_mine, dy_all[0], 0, 0) + contract(g_other, dy_all[1], 0, 0)
        grad_down = take_apart(grad_down, 4, 4, BC)
        du_mine, du_other, grad_down = together(du_mine, du_other, grad_down)
        got_down = data_scatter(grad_down)
        send = contract(du_other, w_up, 1, 1).astype(BF16)
        keep = contract(after(du_mine, send), w_up, 1, 1)
        dc_core = keep, trade(send, "c")
        du_mine, du_other = after((du_mine, du_other), keep)
        grad_up = contract(c_two[0], du_mine, 0, 0) + contract(c_two[1], du_other, 0, 0)
        grad_up = take_apart(grad_up, 8, 2, BC)
        got_up = data_scatter(grad_up)
        dc = scatter_relative(dc_core, grad_up)
        back2, ln2_gain_grad, ln2_shift_grad = norm_back(dc, unit2, inverse2, ln2_gain)
        dh1 = dy.astype(F32) + back2
        da_own, got_down = together(dh1.astype(BF16), got_down)
        g_mine, g_other = after((g_mine, g_other), da_own)
        send = contract(g_other, w_down, 1, 0).astype(BF16)
        keep = contract(g_mine, w_down, 1, 0)
        da_two = gather_relative(da_own, keep)
        do = jnp.stack([contract(rows, w_out, 1, 1).astype(BF16) for rows in da_two])
        do = to_member(do.reshape(2, 2, 2, CH, 2 * DH)).reshape(2 * LEN, 2 * DH)
        dqkv = jnp.concatenate(attend_back(seg_col, seg_row, qkv, do, lse), axis=1)
        dqkv, got_up = together(dqkv, got_up)
        grad_qkv = take_apart(contract(a_all, dqkv, 0, 0), 8, 3, CH)
        mixed_two = to_relative(mixed.reshape(2, 2, 2, CH, 2 * DH)).reshape(2, 4 * CH, 2 * DH)
        mixed_two = after(mixed_two, grad_qkv)
        grad_out = contract(mixed_two[0], da_two[0], 0, 0) + contract(mixed_two[1], da_two[1], 0, 0)
        grad_out = take_apart(grad_out, 1, 8, CH)
        got_first = data_scatter(jnp.concatenate([grad_qkv, grad_out], axis=2))
        dqkv, grad_out = together(dqkv, grad_out)
        da = scatter_chips(scatter_core(dqkv, w_qkv, 1))
        got_rest = grouped(jnp.concatenate([got_up, got_down], axis=1).reshape(-1, rows, BC))
        da, got_rest = together(da, got_rest)
        back1, ln1_gain_grad, ln1_shift_grad = norm_back(da, unit1, inverse1, ln1_gain)
        send, ln1_gain_grad = together(send, ln1_gain_grad)
        branch = keep, trade(send, "c")
        du_sum = jnp.sum(du_mine.astype(F32), axis=0) + jnp.sum(du_other.astype(F32), axis=0)
        dqkv_sum = jnp.sum(dqkv.astype(F32), axis=0)

        def spread(values, size):
            return lax.dynamic_update_slice_in_dim(jnp.zeros((size,), F32), values, member * values.shape[0], 0)

        terms = jnp.stack(
            [
                ln1_gain_grad, ln1_shift_grad, spread(dqkv_sum[:CH], D), spread(dqkv_sum[2 * CH :], D),
                jnp.sum(da_own.astype(F32), axis=0), ln2_gain_grad, ln2_shift_grad,
                jnp.sum(dy.astype(F32), axis=0),
            ],
            axis=1,
        ).reshape(-1)
        terms = jnp.concatenate([terms, spread(du_sum, FF)])
        vector_grads = jnp.sum(everyone(terms.reshape(devices, vector_part)), axis=0)

        got_first, branch, vector_grads, got_rest = together(got_first, branch, vector_grads, got_rest)
        got_first = grouped(got_first.reshape(-1, rows, CH))
        got_first = got_first.reshape(TP, 32, rows, CH)
        got_qkv = got_first[:, :24].reshape(4, 2, 24, rows, CH).transpose(0, 2, 3, 1, 4).reshape(-1, rows, BC)
        got_out = got_first[:, 24:].reshape(TP, 4, 2, rows, CH).transpose(0, 1, 3, 2, 4)
        got_rest = jnp.concatenate(
            [got_out.reshape(TP, 4, rows, BC), got_rest.reshape(TP, 32, rows, BC)], axis=1
        ).reshape(-1, rows, BC)
        got = jnp.concatenate([got_qkv, got_rest], axis=0)
        got = lax.dot_general(got_pick, got, (((0,), (0,)), ((), ())), preferred_element_type=BF16)
        branch, got = together(branch, got)
        owned = everyone(got)
        block_grads = uncut(owned, per_owner).astype(F32)
        branch = scatter_relative(branch)
        out_own = (h1 + branch + down_bias).astype(BF16)
        input_own = (dh1 + back1).astype(BF16)
        head_ids = jnp.arange(HEADS, dtype=jnp.int32)
        tops = jnp.max(tops[:, 0, 0].reshape(2, 2), axis=0)
        tops = jnp.where(head_ids // 2 == member, jnp.where(head_ids % 2 == 0, tops[0], tops[1]), NEG)
        square = jnp.sum(block_grads * block_grads) + jnp.sum(vector_grads * vector_grads)
        square, out_own = together(square, out_own)
        told = jnp.concatenate([tops, square[None], jnp.zeros((128 - HEADS - 1,), F32)])
        told = everyone(jnp.broadcast_to(told[None, None], (devices, 1, 128))).reshape(devices, 128)
        out_own, input_own, told = together(out_own, input_own, told)
        out_tokens = swap_tokens(out_own)
        input_grad = swap_tokens(input_own).astype(F32)
        head_max = jnp.max(told[:, :HEADS], axis=0)
        grad_norm = jnp.sqrt(jnp.sum(told[:, HEADS]))
        total_params = slots.shape[0] * BR * BC + vector_part * devices
        clip = jnp.minimum(1.0, math.sqrt(total_params) / (grad_norm + 1e-06))
        tau = jnp.mean(head_max)
        clip_factors = tau / jnp.maximum(head_max, tau)
        root_factor = jnp.sqrt(clip_factors)
        new_blocks, new_first, new_second, copies = update_blocks(
            clip, column_scale(own_ids, root_factor), block_grads, first_moment, second_moment,
            left_bases, right_bases, blocks,
        )
        vclipped = vector_grads * clip
        new_vector_first = 0.5 * vector_first + 0.5 * vclipped
        new_vector_second = 0.5 * vector_second + 0.5 * vclipped * vclipped
        vupdated = vectors - 0.1 * new_vector_first / (jnp.sqrt(new_vector_second) + 1e-08)
        positions = rank * vector_part + jnp.arange(vector_part, dtype=jnp.int32)
        new_vectors = vupdated * vector_scale(positions, root_factor)
        return (
            out_tokens[None],
            input_grad[None],
            block_grads,
            vector_grads,
            new_blocks,
            new_first,
            new_second,
            copies,
            new_vectors,
            new_vector_first,
            new_vector_second,
            new_vectors.astype(BF16),
            grad_norm,
            clip_factors,
        )

    return local


def solution(mesh):
    outer = mesh.shape["dp"] // 8
    fine = Mesh(mesh.devices.reshape(outer, 2, 2, 2, 2, 2), EVERY)
    seq, pos = ("p", "q", "i", "c"), ("h", "l")
    token, owned, entry = P(seq, pos, None), P(EVERY, None, None), P(EVERY)
    return jax.shard_map(
        make_local(outer),
        mesh=fine,
        in_specs=(token, P(seq, None), token, P(), *[owned] * 5, *[entry] * 3),
        out_specs=(token, token, owned, entry, *[owned] * 4, *[entry] * 4, P(), P()),
        check_vma=False,
    )
```

```python
import functools
import math

import jax
import jax.numpy as jnp
from jax import lax
from jax.experimental import pallas as pl
from jax.experimental.pallas import tpu as pltpu
from jax.sharding import Mesh
from jax.sharding import PartitionSpec as P

D = 2048
HEADS = 16
DH = 128
FF = 8192
BR = 256
BC = 512
TP = 8
LEN = 1024
CH = 256

F32 = jnp.float32
BF16 = jnp.bfloat16
NEG = -1e30
SCALE = DH ** (-0.5)

EVERY = ("p", "q", "i", "c", "h", "l")
GROUP = ("q", "i", "c")
DATA = ("p", "h", "l")


def at(array, index, axis=0):
    return lax.dynamic_index_in_dim(array, index, axis, keepdims=False)


def trade(array, axis):
    return lax.ppermute(array, axis, [(0, 1), (1, 0)])


def after(value, *others):
    return lax.optimization_barrier((value, others))[0]


def together(*values):
    return lax.optimization_barrier(values)


def nothing_of(array):
    return array[(0,) * array.ndim].astype(F32) * 0.0


def swap_tokens(array):
    bits = [(i, c, h, l) for i in range(2) for c in range(2) for h in range(2) for l in range(2)]
    pairs = [(8 * i + 4 * c + 2 * h + l, 8 * l + 4 * h + 2 * c + i) for i, c, h, l in bits]
    other = lax.ppermute(array, ("i", "c", "h", "l"), [pair for pair in pairs if pair[0] != pair[1]])
    i, c, h, l = (lax.axis_index(name) for name in ("i", "c", "h", "l"))
    return jnp.where((i == l) & (c == h), array, other)


def pair_up(array, axis):
    other = trade(array, axis)
    mine = lax.axis_index(axis) == 0
    return jnp.stack([jnp.where(mine, array, other), jnp.where(mine, other, array)])


def group_gather(array):
    return lax.all_gather(array, GROUP, axis=0, tiled=True)


def to_relative(array):
    q, i, c = (lax.axis_index(name) for name in GROUP)
    rows = [at(at(at(array, q ^ m, 0), c ^ n, 0), i ^ k, 0) for n in range(2) for m in range(2) for k in range(2)]
    return jnp.stack(rows).reshape(2, 2, 2, *array.shape[3:])


def to_member(array):
    q, i, c = (lax.axis_index(name) for name in GROUP)
    rows = [at(at(at(array, c ^ n, 0), q ^ m, 0), i ^ k, 0) for m in range(2) for n in range(2) for k in range(2)]
    return jnp.stack(rows).reshape(2, 2, 2, *array.shape[3:])


def gather_relative(own, *fillers):
    first, second = own[:, : D // 2], own[:, D // 2 :]
    first = jnp.stack([first, trade(first, "i")])
    second = jnp.stack([second, trade(second, "q")])
    first_other, second_other = trade(first, "q"), trade(second, "i")
    zero = sum((nothing_of(filler) for filler in fillers), jnp.float32(0)).astype(BF16)
    first = jnp.stack([first, first_other + zero])
    second = jnp.stack([second, second_other + zero]).transpose(1, 0, 2, 3)
    mine = jnp.concatenate([first, second], axis=-1).reshape(4 * CH, D)
    return mine, trade(mine, "c")


def scatter_relative(pair, *fillers):
    total = (pair[0] + pair[1].astype(F32)).astype(BF16).reshape(2, 2, CH, D)
    first, second = total[..., : D // 2], total[..., D // 2 :]
    first_other = trade(first[1], "q")
    second_other = trade(second[:, 1], "i")
    zero = sum((nothing_of(filler) for filler in fillers), jnp.float32(0))
    first = (first[0].astype(F32) + (first_other.astype(F32) + zero)).astype(BF16)
    second = (second[:, 0].astype(F32) + (second_other.astype(F32) + zero)).astype(BF16)
    first_other = trade(first[1], "i")
    second_other = trade(second[1], "q")
    return jnp.concatenate(
        [first[0].astype(F32) + first_other.astype(F32), second[0].astype(F32) + second_other.astype(F32)], axis=1
    )


def scatter_core(left, right, right_dim):
    c = lax.axis_index("c")
    left = left.reshape(2, 2, 2 * CH, -1)
    send = contract(at(left, 1 - c, 1).reshape(4 * CH, -1), right, 1, right_dim).astype(BF16)
    keep = contract(at(left, c, 1).reshape(4 * CH, -1), right, 1, right_dim)
    return keep, trade(send, "c")


def scatter_chips(pair):
    q, i = lax.axis_index("q"), lax.axis_index("i")
    total = (pair[0] + pair[1].astype(F32)).astype(BF16).reshape(2, 2, CH, D)
    first, second = total[..., : D // 2], total[..., D // 2 :]
    first_other = trade(at(first, 1 - q, 0), "q")
    second_other = trade(at(second, 1 - i, 1), "i")
    first = (at(first, q, 0).astype(F32) + first_other.astype(F32)).astype(BF16)
    second = (at(second, i, 1).astype(F32) + second_other.astype(F32)).astype(BF16)
    first_other = trade(at(first, 1 - i), "i")
    second_other = trade(at(second, 1 - q), "q")
    first = at(first, i).astype(F32) + first_other.astype(F32)
    second = at(second, q).astype(F32) + second_other.astype(F32)
    return jnp.concatenate([first, second], axis=1)


def norm_parts(hidden):
    average = jnp.mean(hidden, axis=-1, keepdims=True)
    centred = hidden - average
    variance = jnp.mean(centred * centred, axis=-1, keepdims=True)
    inverse = lax.rsqrt(variance + 1e-05)
    return centred * inverse, inverse


def norm_back(grad, unit, inverse, gain):
    scaled = grad * gain
    inner = jnp.mean(scaled * unit, axis=-1, keepdims=True)
    back = inverse * (scaled - jnp.mean(scaled, axis=-1, keepdims=True) - unit * inner)
    return back, jnp.sum(grad * unit, axis=0), jnp.sum(grad, axis=0)


def contract(left, right, left_dim, right_dim):
    return lax.dot_general(
        left, right, (((left_dim,), (right_dim,)), ((), ())), preferred_element_type=F32
    )


def allowed_pairs(seg_col, seg_row, j, low, high):
    rows = j * CH + lax.broadcasted_iota(jnp.int32, (CH, high - low), 0)
    cols = low + lax.broadcasted_iota(jnp.int32, (CH, high - low), 1)
    same = seg_col[0, j * CH : (j + 1) * CH, :] == seg_row[0, :, low:high]
    return same & (cols <= rows)


def attend_kernel(seg_col, seg_row, q_ref, k_ref, v_ref, o_ref, lse_ref, top_ref):
    top = jnp.full((1, 1), NEG, F32)
    for j in range(LEN // CH):
        low, high = max(0, j - 2) * CH, (j + 1) * CH
        scores = contract(q_ref[j * CH : high, :], k_ref[low:high, :], 1, 1) * SCALE
        scores = jnp.where(allowed_pairs(seg_col, seg_row, j, low, high), scores, NEG)
        peak = jnp.max(scores, axis=-1, keepdims=True)
        weights = jnp.exp(scores - peak)
        total = jnp.sum(weights, axis=-1, keepdims=True)
        probs = (weights * (1.0 / total)).astype(BF16)
        o_ref[j * CH : high, :] = contract(probs, v_ref[low:high, :], 1, 0).astype(BF16)
        lse_ref[0, j * CH : high, :] = peak + jnp.log(total)
        top = jnp.maximum(top, jnp.max(peak, axis=0, keepdims=True))
    top_ref[0] = jnp.broadcast_to(top, (8, 128))


def attend_back_kernel(
    seg_col, seg_row, q_ref, k_ref, v_ref, do_ref, lse_ref, dq_ref, dk_ref, dv_ref, dk_sum, dv_sum
):
    dk_sum[...] = jnp.zeros_like(dk_sum)
    dv_sum[...] = jnp.zeros_like(dv_sum)
    for j in range(LEN // CH):
        low, high = max(0, j - 2) * CH, (j + 1) * CH
        query, keys = q_ref[j * CH : high, :], k_ref[low:high, :]
        grad = do_ref[j * CH : high, :]
        scores = contract(query, keys, 1, 1) * SCALE
        allowed = allowed_pairs(seg_col, seg_row, j, low, high)
        probs = jnp.where(allowed, jnp.exp(scores - lse_ref[0, j * CH : high, :]), 0.0)
        grad_probs = contract(grad, v_ref[low:high, :], 1, 1)
        inner = jnp.sum(probs * grad_probs, axis=-1, keepdims=True)
        grad_scores = (probs * (grad_probs - inner)).astype(BF16)
        dq_ref[j * CH : high, :] = (contract(grad_scores, keys, 1, 0) * SCALE).astype(BF16)
        dk_sum[low:high, :] += contract(grad_scores, query, 0, 0)
        dv_sum[low:high, :] += contract(probs.astype(BF16), grad, 0, 0)
    dk_ref[...] = (dk_sum[...] * SCALE).astype(BF16)
    dv_ref[...] = dv_sum[...].astype(BF16)


def head_specs():
    seg_col = pl.BlockSpec((1, LEN, 1), lambda s, h: (s, 0, 0))
    seg_row = pl.BlockSpec((1, 1, LEN), lambda s, h: (s, 0, 0))
    thirds = [pl.BlockSpec((LEN, DH), lambda s, h, n=n: (s, 2 * n + h)) for n in range(3)]
    lse = pl.BlockSpec((1, LEN, 1), lambda s, h: (2 * s + h, 0, 0))
    return seg_col, seg_row, thirds, lse


def attend(seg_col, seg_row, qkv):
    seg_c, seg_r, thirds, lse = head_specs()
    return pl.pallas_call(
        attend_kernel,
        name="attend",
        grid=(2, 2),
        in_specs=[seg_c, seg_r, *thirds],
        out_specs=[thirds[0], lse, pl.BlockSpec((1, 8, 128), lambda s, h: (2 * s + h, 0, 0))],
        out_shape=[
            jax.ShapeDtypeStruct((2 * LEN, 2 * DH), BF16),
            jax.ShapeDtypeStruct((4, LEN, 1), F32),
            jax.ShapeDtypeStruct((4, 8, 128), F32),
        ],
        compiler_params=pltpu.CompilerParams(vmem_limit_bytes=40 << 20),
        cost_estimate=pl.CostEstimate(flops=1 << 20, bytes_accessed=1 << 10, transcendentals=0),
    )(seg_col, seg_row, qkv, qkv, qkv)


def attend_back(seg_col, seg_row, qkv, grad, lse_all):
    seg_c, seg_r, thirds, lse = head_specs()
    return pl.pallas_call(
        attend_back_kernel,
        name="attend_back",
        grid=(2, 2),
        in_specs=[seg_c, seg_r, *thirds, thirds[0], lse],
        out_specs=[thirds[0]] * 3,
        out_shape=[jax.ShapeDtypeStruct((2 * LEN, 2 * DH), BF16)] * 3,
        scratch_shapes=[pltpu.VMEM((LEN, DH), F32), pltpu.VMEM((LEN, DH), F32)],
        compiler_params=pltpu.CompilerParams(vmem_limit_bytes=40 << 20),
        cost_estimate=pl.CostEstimate(flops=5 << 30, bytes_accessed=8 << 20, transcendentals=1 << 22),
    )(seg_col, seg_row, qkv, qkv, qkv, grad, lse_all)


def lay_out_kernel(fold, in_ref, out_ref):
    parts, _, col_units, rows, width = in_ref.shape
    height, width = parts * rows, width // fold
    for j in range(col_units):
        for k in range(fold):
            piece = in_ref[:, 0, j, :, k * width : (k + 1) * width].reshape(height, width)
            out_ref[k * height : (k + 1) * height, j * width : (j + 1) * width] = piece


def lay_out(full, fold=1):
    parts, row_units, col_units, rows, width = full.shape
    block = (fold * parts * rows, col_units * width // fold)
    shape = (row_units * block[0], block[1])
    return pl.pallas_call(
        functools.partial(lay_out_kernel, fold),
        name="lay_out",
        grid=(row_units,),
        in_specs=[pl.BlockSpec((parts, 1, col_units, rows, width), lambda n: (0, n, 0, 0, 0))],
        out_specs=pl.BlockSpec(block, lambda n: (n, 0)),
        out_shape=jax.ShapeDtypeStruct(shape, BF16),
        compiler_params=pltpu.CompilerParams(vmem_limit_bytes=24 << 20),
        cost_estimate=pl.CostEstimate(flops=0, bytes_accessed=4 * shape[0] * shape[1], transcendentals=0),
    )(full)


def block_tables(owners, per_owner, rank):
    ids = jnp.arange(owners.shape[0], dtype=jnp.int32)
    earlier = (owners[None, :] == owners[:, None]) & (ids[None, :] < ids[:, None])
    slots = owners * per_owner + jnp.sum(earlier.astype(jnp.int32), axis=1)
    mine = rank * per_owner + jnp.arange(per_owner, dtype=jnp.int32)
    own_ids = jnp.sum(jnp.where(slots[None, :] == mine[:, None], ids[None, :], 0), axis=1)
    return slots, own_ids


def column_scale(block_ids, root_factor):
    per_row = 3 * D // BC
    columns = (block_ids % per_row)[:, None] * BC + jnp.arange(BC, dtype=jnp.int32)[None, :]
    head_of = columns % D // DH
    picked = jnp.sum(
        jnp.where(head_of[..., None] == jnp.arange(HEADS, dtype=jnp.int32), root_factor, 0.0), axis=-1
    )
    inside = (block_ids < D // BR * per_row)[:, None] & (columns < 2 * D)
    return jnp.where(inside, picked, 1.0)


def vector_scale(positions, root_factor):
    inside = (positions < 8 * D) & (positions % 8 == 2)
    head_of = positions // 8 // DH
    picked = jnp.sum(
        jnp.where(head_of[:, None] == jnp.arange(HEADS, dtype=jnp.int32), root_factor, 0.0), axis=-1
    )
    return jnp.where(inside, picked, 1.0)


def split3(matrix):
    high = matrix.astype(BF16)
    return high, (matrix - high.astype(F32)).astype(BF16)


def dot3(left, right, right_dim=0):
    (a, b), (c, d) = left, right
    return contract(a, c, 1, right_dim) + (contract(a, d, 1, right_dim) + contract(b, c, 1, right_dim))


def update_kernel(
    clip_ref, scale_ref, grad_ref, first_ref, second_ref, left_ref, right_ref, block_ref,
    new_block_ref, new_first_ref, new_second_ref, copy_ref,
):
    grad = clip_ref[0] * grad_ref[0]
    new_first = 0.5 * first_ref[0] + 0.5 * grad
    new_first_ref[0] = new_first
    left, right = left_ref[0], split3(right_ref[0])
    turned = dot3(split3(left.T), split3(jnp.concatenate([grad, new_first], axis=1)))
    turned = dot3(split3(jnp.concatenate([turned[:, :BC], turned[:, BC:]], axis=0)), right)
    new_second = 0.5 * second_ref[0] + 0.5 * jnp.square(turned[:BR])
    new_second_ref[0] = new_second
    ratio = turned[BR:] / (jnp.sqrt(new_second) + 1e-08)
    back = dot3(split3(dot3(split3(left), split3(ratio))), right, 1)
    new_block = (block_ref[0] - 0.01 * back) * scale_ref[0]
    new_block_ref[0] = new_block
    copy_ref[0] = new_block.astype(BF16)


def update_blocks(clip, scale, grads, first, second, left, right, blocks):
    count = blocks.shape[0]
    one = pl.BlockSpec((1, BR, BC), lambda n: (n, 0, 0))
    whole = jax.ShapeDtypeStruct(blocks.shape, F32)
    return pl.pallas_call(
        update_kernel,
        name="update_blocks",
        grid=(count,),
        in_specs=[
            pl.BlockSpec(memory_space=pltpu.SMEM),
            pl.BlockSpec((1, 1, BC), lambda n: (n, 0, 0)),
            one, one, one,
            pl.BlockSpec((1, BR, BR), lambda n: (n, 0, 0)),
            pl.BlockSpec((1, BC, BC), lambda n: (n, 0, 0)),
            one,
        ],
        out_specs=[one] * 4,
        out_shape=[whole, whole, whole, jax.ShapeDtypeStruct(blocks.shape, BF16)],
        compiler_params=pltpu.CompilerParams(vmem_limit_bytes=40 << 20),
        cost_estimate=pl.CostEstimate(
            flops=count * (18 << 26), bytes_accessed=count * (23 << 18), transcendentals=count << 17
        ),
    )(clip.reshape(1), scale[:, None, :], grads, first, second, left, right, blocks)


def make_local(outer):
    devices = outer * 32
    rows = BR // devices
    qkv_end = D // BR * (3 * D // BC)
    out_end = qkv_end + D // BR * (D // BC)
    up_end = out_end + D // BR * (FF // BC)

    def everyone(array):
        return lax.all_to_all(array, EVERY, 0, 0, tiled=True)

    def grouped(array):
        return lax.all_to_all(array, GROUP, 0, 0, tiled=True)

    def cut(matrices):
        parts = matrices.reshape(matrices.shape[0], outer, 2, 2, 2, 2, 2, rows, BC)
        return parts.transpose(1, 4, 5, 6, 2, 3, 0, 7, 8).reshape(-1, rows, BC)

    def uncut(parts, count):
        parts = parts.reshape(outer, 2, 2, 2, 2, 2, count, rows, BC)
        return parts.transpose(6, 0, 4, 5, 1, 2, 3, 7, 8).reshape(count, BR, BC)

    def assemble(full, row_units, col_units, width):
        full = full.reshape(devices, row_units, col_units, rows, width)
        if rows != 8:
            return full.transpose(1, 0, 3, 2, 4).reshape(row_units * BR, col_units * width)
        return lay_out(full)

    def assemble_qkv(full):
        full = full.reshape(devices, 4, 3, rows, BC)
        if rows != 8:
            full = full.reshape(devices, 4, 3, rows, 2, CH).transpose(1, 4, 0, 3, 2, 5)
            return full.reshape(D, 3 * CH)
        return lay_out(full, 2)

    def take_apart(grad, row_units, col_units, width):
        full = grad.astype(BF16).reshape(row_units, devices, rows, col_units, width)
        full = full.transpose(1, 0, 3, 2, 4)
        return full.reshape(outer * 4, TP, row_units * col_units, rows, width)

    def local(
        tokens, segments, out_grad, owners, blocks, first_moment, second_moment,
        left_bases, right_bases, vectors, vector_first, vector_second,
    ):
        per_owner, vector_part = blocks.shape[0], vectors.shape[0]
        p, q, i, c, h, l = (lax.axis_index(name) for name in EVERY)
        rank = ((((p * 2 + q) * 2 + i) * 2 + c) * 2 + h) * 2 + l
        member = (q * 2 + i) * 2 + c

        def data_gather(piece):
            return lax.all_gather(piece, DATA, axis=0)

        def data_scatter(full):
            return lax.psum_scatter(full, DATA, scatter_dimension=0, tiled=False)

        low = jnp.pad(vectors.astype(BF16), (0, rows * BC - vector_part))
        low = jnp.broadcast_to(low.reshape(1, 1, rows, BC), (devices, 1, rows, BC))
        sent = jnp.concatenate([cut(blocks.astype(BF16)).reshape(devices, per_owner, rows, BC), low], axis=1)
        pieces = everyone(sent.reshape(-1, rows, BC))
        seg = at(at(pair_up(pair_up(segments, "c"), "i"), l), h)
        seg = pair_up(seg, "q").reshape(2, LEN)
        seg_col, seg_row = seg[:, :, None], seg[:, None, :]
        x_low = swap_tokens(tokens.reshape(CH, D))
        dy = swap_tokens(out_grad.reshape(CH, D))
        x_all = group_gather(x_low).reshape(2, 2, 2, CH, D)
        slots, own_ids = block_tables(owners, per_owner, rank)
        rest_order = jnp.concatenate(
            [
                slots[qkv_end:out_end].reshape(TP, -1),
                slots[out_end:up_end].reshape(8, TP, 2).transpose(1, 0, 2).reshape(TP, -1),
                slots[up_end:].reshape(TP, -1),
            ],
            axis=1,
        )
        order = jnp.concatenate(
            [slots[:qkv_end].reshape(8, 3, 4).transpose(2, 0, 1).reshape(-1), rest_order.reshape(-1)]
        )
        order = order + order // per_owner + (nothing_of(seg_row) + nothing_of(x_low) + nothing_of(dy)).astype(jnp.int32)
        got_order = order - order // (per_owner + 1)
        place = jnp.arange(devices * (per_owner + 1), dtype=jnp.int32)
        pick = (order[:, None] == place[None, :]).astype(BF16)
        got_pick = (got_order[:, None] == place[None, : devices * per_owner]).astype(BF16)
        vector_all = pieces.reshape(devices, per_owner + 1, rows * BC)[:, per_owner, :vector_part]
        vector_all = vector_all.reshape(-1).astype(F32)
        feature = vector_all[: 8 * D].reshape(D, 8)
        ln1_gain, ln1_shift, q_bias, v_bias, out_bias, ln2_gain, ln2_shift, down_bias = (
            feature[:, n] for n in range(8)
        )
        up_bias = lax.dynamic_slice_in_dim(vector_all, 8 * D + member * (FF // TP), FF // TP)
        qkv_bias = jnp.concatenate(
            [
                lax.dynamic_slice_in_dim(q_bias, member * CH, CH),
                jnp.zeros((CH,), F32),
                lax.dynamic_slice_in_dim(v_bias, member * CH, CH),
            ]
        )
        pieces = lax.dot_general(pick, pieces, (((1,), (0,)), ((), ())), preferred_element_type=BF16)
        part = pieces[:qkv_end].reshape(4, 4, 2, 3, rows, 2, CH).transpose(0, 5, 1, 3, 4, 2, 6)
        part = jnp.concatenate(
            [part.reshape(TP, 12, rows, BC), pieces[qkv_end:].reshape(TP, 36, rows, BC)], axis=1
        )
        part = grouped(part.reshape(-1, rows, BC)).reshape(TP, 48, rows, BC)
        part, x_all, dy = together(part, x_all, dy)
        w_qkv, part = together(data_gather(part[:, :12]), part)
        w_out = data_gather(part[:, 12:16])
        w_rest = data_gather(part[:, 16:])
        w_qkv = assemble_qkv(w_qkv)
        w_out = assemble(w_out, 1, 4, BC)
        x = x_low.astype(F32)
        unit_all, _ = norm_parts(x_all.reshape(2 * LEN, D).astype(F32))
        a_all = (unit_all * ln1_gain + ln1_shift).astype(BF16)
        a_all = a_all.reshape(2, 2, 2, CH, D).transpose(0, 2, 1, 3, 4).reshape(2 * LEN, D)
        dy_all = gather_relative(dy)
        unit1, inverse1 = norm_parts(x)

        qkv = (jnp.dot(a_all, w_qkv, preferred_element_type=F32) + qkv_bias).astype(BF16)
        mixed, lse, tops = attend(seg_col, seg_row, qkv)
        mixed, *dy_all = together(mixed, *dy_all)
        h1 = x + scatter_chips(scatter_core(mixed, w_out, 0)) + out_bias
        unit2, inverse2 = norm_parts(h1)
        c_own = (unit2 * ln2_gain + ln2_shift).astype(BF16)
        w_up, w_down = w_rest[:, :, :16], w_rest[:, :, 16:]
        w_up = assemble(w_up, 8, 2, BC)
        c_two = gather_relative(c_own)

        u_two = [jnp.dot(tokens_of, w_up, preferred_element_type=F32) + up_bias for tokens_of in c_two]
        def activate(u):
            return (u * (0.5 * (1.0 + lax.erf(u * math.sqrt(0.5))))).astype(BF16)

        g_mine, g_other = activate(u_two[0]), activate(u_two[1])
        grad_down = contract(g_mine, dy_all[0], 0, 0) + contract(g_other, dy_all[1], 0, 0)
        grad_down = take_apart(grad_down, 4, 4, BC)
        u_two[0], u_two[1], w_down, grad_down = together(u_two[0], u_two[1], w_down, grad_down)
        got_down = data_scatter(grad_down)
        w_down = assemble(w_down, 4, 4, BC)

        def back(u, grads):
            slope = 0.5 * (1.0 + lax.erf(u * math.sqrt(0.5)))
            slope = slope + u * jnp.exp(-0.5 * u * u) * (1.0 / math.sqrt(2.0 * math.pi))
            return (contract(grads, w_down, 1, 1) * slope).astype(BF16)

        du_mine, du_other = back(u_two[0], dy_all[0]), back(u_two[1], dy_all[1])
        send = contract(du_other, w_up, 1, 1).astype(BF16)
        keep = contract(after(du_mine, send), w_up, 1, 1)
        dc_core = keep, trade(send, "c")
        du_mine, du_other = after((du_mine, du_other), keep)
        grad_up = contract(c_two[0], du_mine, 0, 0) + contract(c_two[1], du_other, 0, 0)
        grad_up = take_apart(grad_up, 8, 2, BC)
        got_up = data_scatter(grad_up)
        dc = scatter_relative(dc_core, grad_up)
        back2, ln2_gain_grad, ln2_shift_grad = norm_back(dc, unit2, inverse2, ln2_gain)
        dh1 = dy.astype(F32) + back2
        da_own, got_down = together(dh1.astype(BF16), got_down)
        g_mine, g_other = after((g_mine, g_other), da_own)
        send = contract(g_other, w_down, 1, 0).astype(BF16)
        keep = contract(g_mine, w_down, 1, 0)
        da_two = gather_relative(da_own, keep)
        do = jnp.stack([contract(rows, w_out, 1, 1).astype(BF16) for rows in da_two])
        do = to_member(do.reshape(2, 2, 2, CH, 2 * DH)).reshape(2 * LEN, 2 * DH)
        dqkv = jnp.concatenate(attend_back(seg_col, seg_row, qkv, do, lse), axis=1)
        dqkv, got_up = together(dqkv, got_up)
        grad_qkv = take_apart(contract(a_all, dqkv, 0, 0), 8, 3, CH)
        mixed_two = to_relative(mixed.reshape(2, 2, 2, CH, 2 * DH)).reshape(2, 4 * CH, 2 * DH)
        mixed_two = after(mixed_two, grad_qkv)
        grad_out = contract(mixed_two[0], da_two[0], 0, 0) + contract(mixed_two[1], da_two[1], 0, 0)
        grad_out = take_apart(grad_out, 1, 8, CH)
        got_first = data_scatter(jnp.concatenate([grad_qkv, grad_out], axis=2))
        dqkv, grad_out = together(dqkv, grad_out)
        da = scatter_chips(scatter_core(dqkv, w_qkv, 1))
        got_rest = grouped(jnp.concatenate([got_up, got_down], axis=1).reshape(-1, rows, BC))
        da, got_rest = together(da, got_rest)
        back1, ln1_gain_grad, ln1_shift_grad = norm_back(da, unit1, inverse1, ln1_gain)
        send, ln1_gain_grad = together(send, ln1_gain_grad)
        branch = keep, trade(send, "c")
        du_sum = jnp.sum(du_mine.astype(F32), axis=0) + jnp.sum(du_other.astype(F32), axis=0)
        dqkv_sum = jnp.sum(dqkv.astype(F32), axis=0)

        def spread(values, size):
            return lax.dynamic_update_slice_in_dim(jnp.zeros((size,), F32), values, member * values.shape[0], 0)

        terms = jnp.stack(
            [
                ln1_gain_grad, ln1_shift_grad, spread(dqkv_sum[:CH], D), spread(dqkv_sum[2 * CH :], D),
                jnp.sum(da_own.astype(F32), axis=0), ln2_gain_grad, ln2_shift_grad,
                jnp.sum(dy.astype(F32), axis=0),
            ],
            axis=1,
        ).reshape(-1)
        terms = jnp.concatenate([terms, spread(du_sum, FF)])
        vector_grads = jnp.sum(everyone(terms.reshape(devices, vector_part)), axis=0)

        got_first, branch, got_rest = together(got_first, branch, got_rest)
        got_first = grouped(got_first.reshape(-1, rows, CH))
        got_first = got_first.reshape(TP, 32, rows, CH)
        got_qkv = got_first[:, :24].reshape(4, 2, 24, rows, CH).transpose(0, 2, 3, 1, 4).reshape(-1, rows, BC)
        got_out = got_first[:, 24:].reshape(TP, 4, 2, rows, CH).transpose(0, 1, 3, 2, 4)
        got_rest = jnp.concatenate(
            [got_out.reshape(TP, 4, rows, BC), got_rest.reshape(TP, 32, rows, BC)], axis=1
        ).reshape(-1, rows, BC)
        got = jnp.concatenate([got_qkv, got_rest], axis=0)
        got = lax.dot_general(got_pick, got, (((0,), (0,)), ((), ())), preferred_element_type=BF16)
        branch, got = together(branch, got)
        owned = everyone(got)
        block_grads = uncut(owned, per_owner).astype(F32)
        branch = scatter_relative(branch)
        out_own = (h1 + branch + down_bias).astype(BF16)
        input_own = (dh1 + back1).astype(BF16)
        head_ids = jnp.arange(HEADS, dtype=jnp.int32)
        tops = jnp.max(tops[:, 0, 0].reshape(2, 2), axis=0)
        tops = jnp.where(head_ids // 2 == member, jnp.where(head_ids % 2 == 0, tops[0], tops[1]), NEG)
        square = jnp.sum(block_grads * block_grads) + jnp.sum(vector_grads * vector_grads)
        square, out_own = together(square, out_own)
        told = jnp.concatenate([tops, square[None], jnp.zeros((128 - HEADS - 1,), F32)])
        told = everyone(jnp.broadcast_to(told[None, None], (devices, 1, 128))).reshape(devices, 128)
        out_own, input_own, told = together(out_own, input_own, told)
        out_tokens = swap_tokens(out_own)
        input_grad = swap_tokens(input_own).astype(F32)
        head_max = jnp.max(told[:, :HEADS], axis=0)
        grad_norm = jnp.sqrt(jnp.sum(told[:, HEADS]))
        total_params = slots.shape[0] * BR * BC + vector_part * devices
        clip = jnp.minimum(1.0, math.sqrt(total_params) / (grad_norm + 1e-06))
        tau = jnp.mean(head_max)
        clip_factors = tau / jnp.maximum(head_max, tau)
        root_factor = jnp.sqrt(clip_factors)
        new_blocks, new_first, new_second, copies = update_blocks(
            clip, column_scale(own_ids, root_factor), block_grads, first_moment, second_moment,
            left_bases, right_bases, blocks,
        )
        vclipped = vector_grads * clip
        new_vector_first = 0.5 * vector_first + 0.5 * vclipped
        new_vector_second = 0.5 * vector_second + 0.5 * vclipped * vclipped
        vupdated = vectors - 0.1 * new_vector_first / (jnp.sqrt(new_vector_second) + 1e-08)
        positions = rank * vector_part + jnp.arange(vector_part, dtype=jnp.int32)
        new_vectors = vupdated * vector_scale(positions, root_factor)
        return (
            out_tokens[None],
            input_grad[None],
            block_grads,
            vector_grads,
            new_blocks,
            new_first,
            new_second,
            copies,
            new_vectors,
            new_vector_first,
            new_vector_second,
            new_vectors.astype(BF16),
            grad_norm,
            clip_factors,
        )

    return local


def solution(mesh):
    outer = mesh.shape["dp"] // 8
    fine = Mesh(mesh.devices.reshape(outer, 2, 2, 2, 2, 2), EVERY)
    seq, pos = ("p", "q", "i", "c"), ("h", "l")
    token, owned, entry = P(seq, pos, None), P(EVERY, None, None), P(EVERY)
    return jax.shard_map(
        make_local(outer),
        mesh=fine,
        in_specs=(token, P(seq, None), token, P(), *[owned] * 5, *[entry] * 3),
        out_specs=(token, token, owned, entry, *[owned] * 4, *[entry] * 4, P(), P()),
        check_vma=False,
    )
```

```python
import functools
import math

import jax
import jax.numpy as jnp
from jax import lax
from jax.experimental import pallas as pl
from jax.experimental.pallas import tpu as pltpu
from jax.sharding import Mesh
from jax.sharding import PartitionSpec as P

D = 2048
HEADS = 16
DH = 128
FF = 8192
BR = 256
BC = 512
TP = 8
LEN = 1024
CH = 256

F32 = jnp.float32
BF16 = jnp.bfloat16
NEG = -1e30
SCALE = DH ** (-0.5)

EVERY = ("p", "q", "i", "c", "h", "l")
GROUP = ("q", "i", "c")
DATA = ("p", "h", "l")


def at(array, index, axis=0):
    return lax.dynamic_index_in_dim(array, index, axis, keepdims=False)


def trade(array, axis):
    return lax.ppermute(array, axis, [(0, 1), (1, 0)])


def after(value, *others):
    return lax.optimization_barrier((value, others))[0]


def together(*values):
    return lax.optimization_barrier(values)


def nothing_of(array):
    return array[(0,) * array.ndim].astype(F32) * 0.0


def swap_tokens(array):
    bits = [(i, c, h, l) for i in range(2) for c in range(2) for h in range(2) for l in range(2)]
    pairs = [(8 * i + 4 * c + 2 * h + l, 8 * l + 4 * h + 2 * c + i) for i, c, h, l in bits]
    other = lax.ppermute(array, ("i", "c", "h", "l"), [pair for pair in pairs if pair[0] != pair[1]])
    i, c, h, l = (lax.axis_index(name) for name in ("i", "c", "h", "l"))
    return jnp.where((i == l) & (c == h), array, other)


def pair_up(array, axis):
    other = trade(array, axis)
    mine = lax.axis_index(axis) == 0
    return jnp.stack([jnp.where(mine, array, other), jnp.where(mine, other, array)])


def group_gather(array):
    return lax.all_gather(array, GROUP, axis=0, tiled=True)


def to_relative(array):
    q, i, c = (lax.axis_index(name) for name in GROUP)
    rows = [at(at(at(array, q ^ m, 0), c ^ n, 0), i ^ k, 0) for n in range(2) for m in range(2) for k in range(2)]
    return jnp.stack(rows).reshape(2, 2, 2, *array.shape[3:])


def to_member(array):
    q, i, c = (lax.axis_index(name) for name in GROUP)
    rows = [at(at(at(array, c ^ n, 0), q ^ m, 0), i ^ k, 0) for m in range(2) for n in range(2) for k in range(2)]
    return jnp.stack(rows).reshape(2, 2, 2, *array.shape[3:])


def gather_relative(own, *fillers):
    first, second = own[:, : D // 2], own[:, D // 2 :]
    first = jnp.stack([first, trade(first, "i")])
    second = jnp.stack([second, trade(second, "q")])
    first_other, second_other = trade(first, "q"), trade(second, "i")
    zero = sum((nothing_of(filler) for filler in fillers), jnp.float32(0)).astype(BF16)
    first = jnp.stack([first, first_other + zero])
    second = jnp.stack([second, second_other + zero]).transpose(1, 0, 2, 3)
    mine = jnp.concatenate([first, second], axis=-1).reshape(4 * CH, D)
    return mine, trade(mine, "c")


def scatter_relative(pair, *fillers):
    total = (pair[0] + pair[1].astype(F32)).astype(BF16).reshape(2, 2, CH, D)
    first, second = total[..., : D // 2], total[..., D // 2 :]
    first_other = trade(first[1], "q")
    second_other = trade(second[:, 1], "i")
    zero = sum((nothing_of(filler) for filler in fillers), jnp.float32(0))
    first = (first[0].astype(F32) + (first_other.astype(F32) + zero)).astype(BF16)
    second = (second[:, 0].astype(F32) + (second_other.astype(F32) + zero)).astype(BF16)
    first_other = trade(first[1], "i")
    second_other = trade(second[1], "q")
    return jnp.concatenate(
        [first[0].astype(F32) + first_other.astype(F32), second[0].astype(F32) + second_other.astype(F32)], axis=1
    )


def scatter_core(left, right, right_dim):
    c = lax.axis_index("c")
    left = left.reshape(2, 2, 2 * CH, -1)
    send = contract(at(left, 1 - c, 1).reshape(4 * CH, -1), right, 1, right_dim).astype(BF16)
    keep = contract(at(left, c, 1).reshape(4 * CH, -1), right, 1, right_dim)
    return keep, trade(send, "c")


def scatter_chips(pair):
    q, i = lax.axis_index("q"), lax.axis_index("i")
    total = (pair[0] + pair[1].astype(F32)).astype(BF16).reshape(2, 2, CH, D)
    first, second = total[..., : D // 2], total[..., D // 2 :]
    first_other = trade(at(first, 1 - q, 0), "q")
    second_other = trade(at(second, 1 - i, 1), "i")
    first = (at(first, q, 0).astype(F32) + first_other.astype(F32)).astype(BF16)
    second = (at(second, i, 1).astype(F32) + second_other.astype(F32)).astype(BF16)
    first_other = trade(at(first, 1 - i), "i")
    second_other = trade(at(second, 1 - q), "q")
    first = at(first, i).astype(F32) + first_other.astype(F32)
    second = at(second, q).astype(F32) + second_other.astype(F32)
    return jnp.concatenate([first, second], axis=1)


def norm_parts(hidden):
    average = jnp.mean(hidden, axis=-1, keepdims=True)
    centred = hidden - average
    variance = jnp.mean(centred * centred, axis=-1, keepdims=True)
    inverse = lax.rsqrt(variance + 1e-05)
    return centred * inverse, inverse


def norm_back(grad, unit, inverse, gain):
    scaled = grad * gain
    inner = jnp.mean(scaled * unit, axis=-1, keepdims=True)
    back = inverse * (scaled - jnp.mean(scaled, axis=-1, keepdims=True) - unit * inner)
    return back, jnp.sum(grad * unit, axis=0), jnp.sum(grad, axis=0)


def contract(left, right, left_dim, right_dim):
    return lax.dot_general(
        left, right, (((left_dim,), (right_dim,)), ((), ())), preferred_element_type=F32
    )


def allowed_pairs(seg_col, seg_row, j, low, high):
    rows = j * CH + lax.broadcasted_iota(jnp.int32, (CH, high - low), 0)
    cols = low + lax.broadcasted_iota(jnp.int32, (CH, high - low), 1)
    same = seg_col[0, j * CH : (j + 1) * CH, :] == seg_row[0, :, low:high]
    return same & (cols <= rows)


def attend_kernel(seg_col, seg_row, q_ref, k_ref, v_ref, o_ref, lse_ref, top_ref):
    top = jnp.full((1, 1), NEG, F32)
    for j in range(LEN // CH):
        low, high = max(0, j - 2) * CH, (j + 1) * CH
        scores = contract(q_ref[j * CH : high, :], k_ref[low:high, :], 1, 1) * SCALE
        scores = jnp.where(allowed_pairs(seg_col, seg_row, j, low, high), scores, NEG)
        peak = jnp.max(scores, axis=-1, keepdims=True)
        weights = jnp.exp(scores - peak)
        total = jnp.sum(weights, axis=-1, keepdims=True)
        probs = (weights * (1.0 / total)).astype(BF16)
        o_ref[j * CH : high, :] = contract(probs, v_ref[low:high, :], 1, 0).astype(BF16)
        lse_ref[0, j * CH : high, :] = peak + jnp.log(total)
        top = jnp.maximum(top, jnp.max(peak, axis=0, keepdims=True))
    top_ref[0] = jnp.broadcast_to(top, (8, 128))


def attend_back_kernel(
    seg_col, seg_row, q_ref, k_ref, v_ref, do_ref, lse_ref, dq_ref, dk_ref, dv_ref, dk_sum, dv_sum
):
    dk_sum[...] = jnp.zeros_like(dk_sum)
    dv_sum[...] = jnp.zeros_like(dv_sum)
    for j in range(LEN // CH):
        low, high = max(0, j - 2) * CH, (j + 1) * CH
        query, keys = q_ref[j * CH : high, :], k_ref[low:high, :]
        grad = do_ref[j * CH : high, :]
        scores = contract(query, keys, 1, 1) * SCALE
        allowed = allowed_pairs(seg_col, seg_row, j, low, high)
        probs = jnp.where(allowed, jnp.exp(scores - lse_ref[0, j * CH : high, :]), 0.0)
        grad_probs = contract(grad, v_ref[low:high, :], 1, 1)
        inner = jnp.sum(probs * grad_probs, axis=-1, keepdims=True)
        grad_scores = (probs * (grad_probs - inner)).astype(BF16)
        dq_ref[j * CH : high, :] = (contract(grad_scores, keys, 1, 0) * SCALE).astype(BF16)
        dk_sum[low:high, :] += contract(grad_scores, query, 0, 0)
        dv_sum[low:high, :] += contract(probs.astype(BF16), grad, 0, 0)
    dk_ref[...] = (dk_sum[...] * SCALE).astype(BF16)
    dv_ref[...] = dv_sum[...].astype(BF16)


def head_specs():
    seg_col = pl.BlockSpec((1, LEN, 1), lambda s, h: (s, 0, 0))
    seg_row = pl.BlockSpec((1, 1, LEN), lambda s, h: (s, 0, 0))
    thirds = [pl.BlockSpec((LEN, DH), lambda s, h, n=n: (s, 2 * n + h)) for n in range(3)]
    lse = pl.BlockSpec((1, LEN, 1), lambda s, h: (2 * s + h, 0, 0))
    return seg_col, seg_row, thirds, lse


def attend(seg_col, seg_row, qkv):
    seg_c, seg_r, thirds, lse = head_specs()
    return pl.pallas_call(
        attend_kernel,
        name="attend",
        grid=(2, 2),
        in_specs=[seg_c, seg_r, *thirds],
        out_specs=[thirds[0], lse, pl.BlockSpec((1, 8, 128), lambda s, h: (2 * s + h, 0, 0))],
        out_shape=[
            jax.ShapeDtypeStruct((2 * LEN, 2 * DH), BF16),
            jax.ShapeDtypeStruct((4, LEN, 1), F32),
            jax.ShapeDtypeStruct((4, 8, 128), F32),
        ],
        compiler_params=pltpu.CompilerParams(vmem_limit_bytes=40 << 20),
        cost_estimate=pl.CostEstimate(flops=1 << 20, bytes_accessed=1 << 10, transcendentals=0),
    )(seg_col, seg_row, qkv, qkv, qkv)


def attend_back(seg_col, seg_row, qkv, grad, lse_all):
    seg_c, seg_r, thirds, lse = head_specs()
    return pl.pallas_call(
        attend_back_kernel,
        name="attend_back",
        grid=(2, 2),
        in_specs=[seg_c, seg_r, *thirds, thirds[0], lse],
        out_specs=[thirds[0]] * 3,
        out_shape=[jax.ShapeDtypeStruct((2 * LEN, 2 * DH), BF16)] * 3,
        scratch_shapes=[pltpu.VMEM((LEN, DH), F32), pltpu.VMEM((LEN, DH), F32)],
        compiler_params=pltpu.CompilerParams(vmem_limit_bytes=40 << 20),
        cost_estimate=pl.CostEstimate(flops=5 << 30, bytes_accessed=8 << 20, transcendentals=1 << 22),
    )(seg_col, seg_row, qkv, qkv, qkv, grad, lse_all)


def lay_out_kernel(fold, in_ref, out_ref):
    parts, _, col_units, rows, width = in_ref.shape
    height, width = parts * rows, width // fold
    for j in range(col_units):
        for k in range(fold):
            piece = in_ref[:, 0, j, :, k * width : (k + 1) * width].reshape(height, width)
            out_ref[k * height : (k + 1) * height, j * width : (j + 1) * width] = piece


def lay_out(full, fold=1):
    parts, row_units, col_units, rows, width = full.shape
    block = (fold * parts * rows, col_units * width // fold)
    shape = (row_units * block[0], block[1])
    return pl.pallas_call(
        functools.partial(lay_out_kernel, fold),
        name="lay_out",
        grid=(row_units,),
        in_specs=[pl.BlockSpec((parts, 1, col_units, rows, width), lambda n: (0, n, 0, 0, 0))],
        out_specs=pl.BlockSpec(block, lambda n: (n, 0)),
        out_shape=jax.ShapeDtypeStruct(shape, BF16),
        compiler_params=pltpu.CompilerParams(vmem_limit_bytes=24 << 20),
        cost_estimate=pl.CostEstimate(flops=0, bytes_accessed=4 * shape[0] * shape[1], transcendentals=0),
    )(full)


def block_tables(owners, per_owner, rank):
    ids = jnp.arange(owners.shape[0], dtype=jnp.int32)
    earlier = (owners[None, :] == owners[:, None]) & (ids[None, :] < ids[:, None])
    slots = owners * per_owner + jnp.sum(earlier.astype(jnp.int32), axis=1)
    mine = rank * per_owner + jnp.arange(per_owner, dtype=jnp.int32)
    own_ids = jnp.sum(jnp.where(slots[None, :] == mine[:, None], ids[None, :], 0), axis=1)
    return slots, own_ids


def column_scale(block_ids, root_factor):
    per_row = 3 * D // BC
    columns = (block_ids % per_row)[:, None] * BC + jnp.arange(BC, dtype=jnp.int32)[None, :]
    head_of = columns % D // DH
    picked = jnp.sum(
        jnp.where(head_of[..., None] == jnp.arange(HEADS, dtype=jnp.int32), root_factor, 0.0), axis=-1
    )
    inside = (block_ids < D // BR * per_row)[:, None] & (columns < 2 * D)
    return jnp.where(inside, picked, 1.0)


def vector_scale(positions, root_factor):
    inside = (positions < 8 * D) & (positions % 8 == 2)
    head_of = positions // 8 // DH
    picked = jnp.sum(
        jnp.where(head_of[:, None] == jnp.arange(HEADS, dtype=jnp.int32), root_factor, 0.0), axis=-1
    )
    return jnp.where(inside, picked, 1.0)


def split3(matrix):
    high = matrix.astype(BF16)
    return high, (matrix - high.astype(F32)).astype(BF16)


def dot3(left, right, right_dim=0):
    (a, b), (c, d) = left, right
    return contract(a, c, 1, right_dim) + (contract(a, d, 1, right_dim) + contract(b, c, 1, right_dim))


def update_kernel(
    clip_ref, scale_ref, grad_ref, first_ref, second_ref, left_ref, right_ref, block_ref,
    new_block_ref, new_first_ref, new_second_ref, copy_ref,
):
    grad = clip_ref[0] * grad_ref[0]
    new_first = 0.5 * first_ref[0] + 0.5 * grad
    new_first_ref[0] = new_first
    left, right = left_ref[0], split3(right_ref[0])
    turned = dot3(split3(left.T), split3(jnp.concatenate([grad, new_first], axis=1)))
    turned = dot3(split3(jnp.concatenate([turned[:, :BC], turned[:, BC:]], axis=0)), right)
    new_second = 0.5 * second_ref[0] + 0.5 * jnp.square(turned[:BR])
    new_second_ref[0] = new_second
    ratio = turned[BR:] / (jnp.sqrt(new_second) + 1e-08)
    back = dot3(split3(dot3(split3(left), split3(ratio))), right, 1)
    new_block = (block_ref[0] - 0.01 * back) * scale_ref[0]
    new_block_ref[0] = new_block
    copy_ref[0] = new_block.astype(BF16)


def update_blocks(clip, scale, grads, first, second, left, right, blocks):
    count = blocks.shape[0]
    one = pl.BlockSpec((1, BR, BC), lambda n: (n, 0, 0))
    whole = jax.ShapeDtypeStruct(blocks.shape, F32)
    return pl.pallas_call(
        update_kernel,
        name="update_blocks",
        grid=(count,),
        in_specs=[
            pl.BlockSpec(memory_space=pltpu.SMEM),
            pl.BlockSpec((1, 1, BC), lambda n: (n, 0, 0)),
            one, one, one,
            pl.BlockSpec((1, BR, BR), lambda n: (n, 0, 0)),
            pl.BlockSpec((1, BC, BC), lambda n: (n, 0, 0)),
            one,
        ],
        out_specs=[one] * 4,
        out_shape=[whole, whole, whole, jax.ShapeDtypeStruct(blocks.shape, BF16)],
        compiler_params=pltpu.CompilerParams(vmem_limit_bytes=40 << 20),
        cost_estimate=pl.CostEstimate(
            flops=count * (18 << 26), bytes_accessed=count * (23 << 18), transcendentals=count << 17
        ),
    )(clip.reshape(1), scale[:, None, :], grads, first, second, left, right, blocks)


def make_local(outer):
    devices = outer * 32
    rows = BR // devices
    qkv_end = D // BR * (3 * D // BC)
    out_end = qkv_end + D // BR * (D // BC)
    up_end = out_end + D // BR * (FF // BC)

    def everyone(array):
        return lax.all_to_all(array, EVERY, 0, 0, tiled=True)

    def grouped(array):
        return lax.all_to_all(array, GROUP, 0, 0, tiled=True)

    def cut(matrices):
        parts = matrices.reshape(matrices.shape[0], outer, 2, 2, 2, 2, 2, rows, BC)
        return parts.transpose(1, 4, 5, 6, 2, 3, 0, 7, 8).reshape(-1, rows, BC)

    def uncut(parts, count):
        parts = parts.reshape(outer, 2, 2, 2, 2, 2, count, rows, BC)
        return parts.transpose(6, 0, 4, 5, 1, 2, 3, 7, 8).reshape(count, BR, BC)

    def assemble(full, row_units, col_units, width):
        full = full.reshape(devices, row_units, col_units, rows, width)
        if rows != 8:
            return full.transpose(1, 0, 3, 2, 4).reshape(row_units * BR, col_units * width)
        return lay_out(full)

    def assemble_qkv(full):
        full = full.reshape(devices, 4, 3, rows, BC)
        if rows != 8:
            full = full.reshape(devices, 4, 3, rows, 2, CH).transpose(1, 4, 0, 3, 2, 5)
            return full.reshape(D, 3 * CH)
        return lay_out(full, 2)

    def take_apart(grad, row_units, col_units, width):
        full = grad.astype(BF16).reshape(row_units, devices, rows, col_units, width)
        full = full.transpose(1, 0, 3, 2, 4)
        return full.reshape(outer * 4, TP, row_units * col_units, rows, width)

    def local(
        tokens, segments, out_grad, owners, blocks, first_moment, second_moment,
        left_bases, right_bases, vectors, vector_first, vector_second,
    ):
        per_owner, vector_part = blocks.shape[0], vectors.shape[0]
        p, q, i, c, h, l = (lax.axis_index(name) for name in EVERY)
        rank = ((((p * 2 + q) * 2 + i) * 2 + c) * 2 + h) * 2 + l
        member = (q * 2 + i) * 2 + c

        def data_gather(piece):
            return lax.all_gather(piece, DATA, axis=0)

        def data_scatter(full):
            return lax.psum_scatter(full, DATA, scatter_dimension=0, tiled=False)

        low = jnp.pad(vectors.astype(BF16), (0, rows * BC - vector_part))
        low = jnp.broadcast_to(low.reshape(1, 1, rows, BC), (devices, 1, rows, BC))
        sent = jnp.concatenate([cut(blocks.astype(BF16)).reshape(devices, per_owner, rows, BC), low], axis=1)
        pieces = everyone(sent.reshape(-1, rows, BC))
        seg = at(at(pair_up(pair_up(segments, "c"), "i"), l), h)
        seg = pair_up(seg, "q").reshape(2, LEN)
        seg_col, seg_row = seg[:, :, None], seg[:, None, :]
        x_low = swap_tokens(tokens.reshape(CH, D))
        dy = swap_tokens(out_grad.reshape(CH, D))
        x_all = group_gather(x_low).reshape(2, 2, 2, CH, D)
        slots, own_ids = block_tables(owners, per_owner, rank)
        rest_order = jnp.concatenate(
            [
                slots[qkv_end:out_end].reshape(TP, -1),
                slots[out_end:up_end].reshape(8, TP, 2).transpose(1, 0, 2).reshape(TP, -1),
                slots[up_end:].reshape(TP, -1),
            ],
            axis=1,
        )
        order = jnp.concatenate(
            [slots[:qkv_end].reshape(8, 3, 4).transpose(2, 0, 1).reshape(-1), rest_order.reshape(-1)]
        )
        order = order + order // per_owner + (nothing_of(seg_row) + nothing_of(x_low) + nothing_of(dy)).astype(jnp.int32)
        got_order = order - order // (per_owner + 1)
        place = jnp.arange(devices * (per_owner + 1), dtype=jnp.int32)
        pick = (order[:, None] == place[None, :]).astype(BF16)
        got_pick = (got_order[:, None] == place[None, : devices * per_owner]).astype(BF16)
        vector_all = pieces.reshape(devices, per_owner + 1, rows * BC)[:, per_owner, :vector_part]
        vector_all = vector_all.reshape(-1).astype(F32)
        feature = vector_all[: 8 * D].reshape(D, 8)
        ln1_gain, ln1_shift, q_bias, v_bias, out_bias, ln2_gain, ln2_shift, down_bias = (
            feature[:, n] for n in range(8)
        )
        up_bias = lax.dynamic_slice_in_dim(vector_all, 8 * D + member * (FF // TP), FF // TP)
        qkv_bias = jnp.concatenate(
            [
                lax.dynamic_slice_in_dim(q_bias, member * CH, CH),
                jnp.zeros((CH,), F32),
                lax.dynamic_slice_in_dim(v_bias, member * CH, CH),
            ]
        )
        pieces = lax.dot_general(pick, pieces, (((1,), (0,)), ((), ())), preferred_element_type=BF16)
        part = pieces[:qkv_end].reshape(4, 4, 2, 3, rows, 2, CH).transpose(0, 5, 1, 3, 4, 2, 6)
        part = jnp.concatenate(
            [part.reshape(TP, 12, rows, BC), pieces[qkv_end:].reshape(TP, 36, rows, BC)], axis=1
        )
        part = grouped(part.reshape(-1, rows, BC)).reshape(TP, 48, rows, BC)
        part, x_all, dy = together(part, x_all, dy)
        w_first, part = together(data_gather(part[:, :16]), part)
        w_qkv, w_out = w_first[:, :, :12], w_first[:, :, 12:]
        w_rest = data_gather(part[:, 16:])
        w_qkv = assemble_qkv(w_qkv)
        w_out = assemble(w_out, 1, 4, BC)
        x = x_low.astype(F32)
        unit_all, _ = norm_parts(x_all.reshape(2 * LEN, D).astype(F32))
        a_all = (unit_all * ln1_gain + ln1_shift).astype(BF16)
        a_all = a_all.reshape(2, 2, 2, CH, D).transpose(0, 2, 1, 3, 4).reshape(2 * LEN, D)
        dy_all = gather_relative(dy)
        unit1, inverse1 = norm_parts(x)

        qkv = (jnp.dot(a_all, w_qkv, preferred_element_type=F32) + qkv_bias).astype(BF16)
        mixed, lse, tops = attend(seg_col, seg_row, qkv)
        mixed, *dy_all = together(mixed, *dy_all)
        h1 = x + scatter_chips(scatter_core(mixed, w_out, 0)) + out_bias
        unit2, inverse2 = norm_parts(h1)
        c_own = (unit2 * ln2_gain + ln2_shift).astype(BF16)
        w_up, w_down = w_rest[:, :, :16], w_rest[:, :, 16:]
        w_up = assemble(w_up, 8, 2, BC)
        c_two = gather_relative(c_own, w_rest)

        u_two = [jnp.dot(tokens_of, w_up, preferred_element_type=F32) + up_bias for tokens_of in c_two]
        def activate(u):
            return (u * (0.5 * (1.0 + lax.erf(u * math.sqrt(0.5))))).astype(BF16)

        g_mine, g_other = activate(u_two[0]), activate(u_two[1])
        grad_down = contract(g_mine, dy_all[0], 0, 0) + contract(g_other, dy_all[1], 0, 0)
        grad_down = take_apart(grad_down, 4, 4, BC)
        u_two[0], u_two[1], w_down, grad_down = together(u_two[0], u_two[1], w_down, grad_down)
        got_down = data_scatter(grad_down)
        w_down = assemble(w_down, 4, 4, BC)

        def back(u, grads):
            slope = 0.5 * (1.0 + lax.erf(u * math.sqrt(0.5)))
            slope = slope + u * jnp.exp(-0.5 * u * u) * (1.0 / math.sqrt(2.0 * math.pi))
            return (contract(grads, w_down, 1, 1) * slope).astype(BF16)

        du_mine, du_other = back(u_two[0], dy_all[0]), back(u_two[1], dy_all[1])
        send = contract(du_other, w_up, 1, 1).astype(BF16)
        keep = contract(after(du_mine, send), w_up, 1, 1)
        dc_core = keep, trade(send, "c")
        du_mine, du_other = after((du_mine, du_other), keep)
        grad_up = contract(c_two[0], du_mine, 0, 0) + contract(c_two[1], du_other, 0, 0)
        grad_up = take_apart(grad_up, 8, 2, BC)
        got_up = data_scatter(grad_up)
        dc = scatter_relative(dc_core, grad_up)
        back2, ln2_gain_grad, ln2_shift_grad = norm_back(dc, unit2, inverse2, ln2_gain)
        dh1 = dy.astype(F32) + back2
        da_own, got_down = together(dh1.astype(BF16), got_down)
        g_mine, g_other = after((g_mine, g_other), da_own)
        send = contract(g_other, w_down, 1, 0).astype(BF16)
        keep = contract(g_mine, w_down, 1, 0)
        da_two = gather_relative(da_own, keep)
        do = jnp.stack([contract(rows, w_out, 1, 1).astype(BF16) for rows in da_two])
        do = to_member(do.reshape(2, 2, 2, CH, 2 * DH)).reshape(2 * LEN, 2 * DH)
        dqkv = jnp.concatenate(attend_back(seg_col, seg_row, qkv, do, lse), axis=1)
        dqkv, got_up = together(dqkv, got_up)
        grad_qkv = take_apart(contract(a_all, dqkv, 0, 0), 8, 3, CH)
        mixed_two = to_relative(mixed.reshape(2, 2, 2, CH, 2 * DH)).reshape(2, 4 * CH, 2 * DH)
        mixed_two = after(mixed_two, grad_qkv)
        grad_out = contract(mixed_two[0], da_two[0], 0, 0) + contract(mixed_two[1], da_two[1], 0, 0)
        grad_out = take_apart(grad_out, 1, 8, CH)
        got_first = data_scatter(jnp.concatenate([grad_qkv, grad_out], axis=2))
        dqkv, grad_out = together(dqkv, grad_out)
        da = scatter_chips(scatter_core(dqkv, w_qkv, 1))
        got_rest = grouped(jnp.concatenate([got_up, got_down], axis=1).reshape(-1, rows, BC))
        da, got_rest = together(da, got_rest)
        back1, ln1_gain_grad, ln1_shift_grad = norm_back(da, unit1, inverse1, ln1_gain)
        send, ln1_gain_grad = together(send, ln1_gain_grad)
        branch = keep, trade(send, "c")
        du_sum = jnp.sum(du_mine.astype(F32), axis=0) + jnp.sum(du_other.astype(F32), axis=0)
        dqkv_sum = jnp.sum(dqkv.astype(F32), axis=0)

        def spread(values, size):
            return lax.dynamic_update_slice_in_dim(jnp.zeros((size,), F32), values, member * values.shape[0], 0)

        terms = jnp.stack(
            [
                ln1_gain_grad, ln1_shift_grad, spread(dqkv_sum[:CH], D), spread(dqkv_sum[2 * CH :], D),
                jnp.sum(da_own.astype(F32), axis=0), ln2_gain_grad, ln2_shift_grad,
                jnp.sum(dy.astype(F32), axis=0),
            ],
            axis=1,
        ).reshape(-1)
        terms = jnp.concatenate([terms, spread(du_sum, FF)])
        vector_grads = jnp.sum(everyone(terms.reshape(devices, vector_part)), axis=0)

        got_first, branch, got_rest = together(got_first, branch, got_rest)
        got_first = grouped(got_first.reshape(-1, rows, CH))
        got_first = got_first.reshape(TP, 32, rows, CH)
        got_qkv = got_first[:, :24].reshape(4, 2, 24, rows, CH).transpose(0, 2, 3, 1, 4).reshape(-1, rows, BC)
        got_out = got_first[:, 24:].reshape(TP, 4, 2, rows, CH).transpose(0, 1, 3, 2, 4)
        got_rest = jnp.concatenate(
            [got_out.reshape(TP, 4, rows, BC), got_rest.reshape(TP, 32, rows, BC)], axis=1
        ).reshape(-1, rows, BC)
        got = jnp.concatenate([got_qkv, got_rest], axis=0)
        got = lax.dot_general(got_pick, got, (((0,), (0,)), ((), ())), preferred_element_type=BF16)
        branch, got = together(branch, got)
        owned = everyone(got)
        block_grads = uncut(owned, per_owner).astype(F32)
        branch = scatter_relative(branch)
        out_own = (h1 + branch + down_bias).astype(BF16)
        input_own = (dh1 + back1).astype(BF16)
        head_ids = jnp.arange(HEADS, dtype=jnp.int32)
        tops = jnp.max(tops[:, 0, 0].reshape(2, 2), axis=0)
        tops = jnp.where(head_ids // 2 == member, jnp.where(head_ids % 2 == 0, tops[0], tops[1]), NEG)
        square = jnp.sum(block_grads * block_grads) + jnp.sum(vector_grads * vector_grads)
        square, out_own = together(square, out_own)
        told = jnp.concatenate([tops, square[None], jnp.zeros((128 - HEADS - 1,), F32)])
        told = everyone(jnp.broadcast_to(told[None, None], (devices, 1, 128))).reshape(devices, 128)
        out_own, input_own, told = together(out_own, input_own, told)
        out_tokens = swap_tokens(out_own)
        input_grad = swap_tokens(input_own).astype(F32)
        head_max = jnp.max(told[:, :HEADS], axis=0)
        grad_norm = jnp.sqrt(jnp.sum(told[:, HEADS]))
        total_params = slots.shape[0] * BR * BC + vector_part * devices
        clip = jnp.minimum(1.0, math.sqrt(total_params) / (grad_norm + 1e-06))
        tau = jnp.mean(head_max)
        clip_factors = tau / jnp.maximum(head_max, tau)
        root_factor = jnp.sqrt(clip_factors)
        new_blocks, new_first, new_second, copies = update_blocks(
            clip, column_scale(own_ids, root_factor), block_grads, first_moment, second_moment,
            left_bases, right_bases, blocks,
        )
        vclipped = vector_grads * clip
        new_vector_first = 0.5 * vector_first + 0.5 * vclipped
        new_vector_second = 0.5 * vector_second + 0.5 * vclipped * vclipped
        vupdated = vectors - 0.1 * new_vector_first / (jnp.sqrt(new_vector_second) + 1e-08)
        positions = rank * vector_part + jnp.arange(vector_part, dtype=jnp.int32)
        new_vectors = vupdated * vector_scale(positions, root_factor)
        return (
            out_tokens[None],
            input_grad[None],
            block_grads,
            vector_grads,
            new_blocks,
            new_first,
            new_second,
            copies,
            new_vectors,
            new_vector_first,
            new_vector_second,
            new_vectors.astype(BF16),
            grad_norm,
            clip_factors,
        )

    return local


def solution(mesh):
    outer = mesh.shape["dp"] // 8
    fine = Mesh(mesh.devices.reshape(outer, 2, 2, 2, 2, 2), EVERY)
    seq, pos = ("p", "q", "i", "c"), ("h", "l")
    token, owned, entry = P(seq, pos, None), P(EVERY, None, None), P(EVERY)
    return jax.shard_map(
        make_local(outer),
        mesh=fine,
        in_specs=(token, P(seq, None), token, P(), *[owned] * 5, *[entry] * 3),
        out_specs=(token, token, owned, entry, *[owned] * 4, *[entry] * 4, P(), P()),
        check_vma=False,
    )
```
